32 devices in a mesh: grp: 2 (over y), frm: 8 (over z, x), tp: 2 (over core).
Axes of the slice: x: 2, y: 2, z: 4, core: 2. Of those that a mesh axis runs over, the one named last changes fastest.
Arguments:
- queries: bfloat16 [3072, 2560], P(('grp', 'frm'), 'tp'), parts along dimension 0, may hold values from -60 to 60, as said below
- key_rows: bfloat16 [3072, 2560], P(('grp', 'frm'), 'tp'), parts along dimension 0, may hold values from -60 to 60
- values: bfloat16 [3072, 2560], P(('grp', 'frm'), 'tp'), parts along dimension 0, may hold values from -6 to 6
- query_gain: float32 [2560], P('tp'), may hold values from 0.25 to 1.75
- key_gain: float32 [2560], P('tp'), may hold values from 0.25 to 1.75
- pattern: int32 [16, 4], P(('grp', 'frm')), parts along dimension 0, may hold values 0 or 1
- reference_keys: bfloat16 [64, 2560], P(('grp', 'frm'), 'tp'), parts along dimension 0, may hold values from -6 to 6
- reference_values: bfloat16 [64, 2560], P(('grp', 'frm'), 'tp'), parts along dimension 0, may hold values from -6 to 6
- reference_live: int32 [16], P(('grp', 'frm')), parts along dimension 0, may hold values from 1 to 4
Outputs:
- attention: bfloat16 [3072, 2560], P(('grp', 'frm'), 'tp'), parts along dimension 0
The draws below stay inside these ranges and needn't reach their ends.
There are 2 independent parts, one for each index of `grp`. The reference program is written for one: setup_inputs(seed, part) draws one part's arguments, and reference() takes and returns one part's arrays. A program takes and returns all parts, laid end to end along the dimension named above; an argument that names none is the same for every part. Nothing has to cross between parts.
Inputs may be any that keep to these rules, and one draw needn't show every extreme that they name: `queries`: query entries lie within the range.
All inputs are finite; a program needn't handle non-finite values. No bound on the sum of `pattern` on one device may be relied on, other than what follows from the above.
Results may differ from the reference program's by a relative error of at most 0.012.
The reference program's roundings to bfloat16 on the way (of `normed_queries`, `normed_keys`, `all_keys`, `all_values` and `rounded`) count: a program that leaves them out, or rounds other values in their place, can miss the bound.
Values may be sent and summed in bfloat16 or wider, within the bound.
No kernel may reach another device: no remote copies, remote signals or barrier semaphores. Data moves between devices by JAX's collectives and lax.ppermute only.
A program may use at most 64 MiB of HBM per device.

```python
import jax
import jax.numpy as jnp
from jax import lax

HEADS = 20
HEAD_DIM = 128
WINDOW = 2
TOK_DEV = 192
REF_DEV = 4
BLOCKS = 8
TOKENS = 1536
REF = 32
D_ATT = 2560


def draw_pair(key, choose_keys):
    base_key = jax.random.fold_in(key, 101)
    row_key, jitter_key = jax.random.split(base_key, 2)
    own_key = jax.random.fold_in(jitter_key, choose_keys)
    scale_key = jax.random.fold_in(row_key, choose_keys)
    columns = HEADS * HEAD_DIM
    head_of = jnp.arange(columns) // HEAD_DIM
    column_scale = 3.0 ** (head_of.astype(jnp.float32) / max(HEADS - 1, 1))
    row_scale = 10.0 ** jax.random.uniform(scale_key, (TOKENS, 1), dtype=jnp.float32)
    jitter = jnp.clip(jax.random.normal(own_key, (TOKENS, columns), dtype=jnp.float32), -4.0, 4.0)
    result = jitter * row_scale * column_scale[None, :]
    return jnp.clip(result, -60.0, 60.0).astype(jnp.bfloat16)


def draw_queries(key, part):
    return draw_pair(key, 0)


def draw_key_rows(key, part):
    return draw_pair(key, 1)


def touch_ends(drawn, rng, least, high):
    dims = drawn.shape
    place = [jax.random.randint(jax.random.fold_in(rng, axis), (), 0, dims[axis]) for axis in range(len(dims))]
    drawn = drawn.at[tuple(place)].set(least)
    longest = dims.index(max(dims))
    place[longest] = (place[longest] + 1) % dims[longest]
    return drawn.at[tuple(place)].set(high)


def level_of(rng, dims, cuts, low, top_value):
    loudness, own = 1.0, jax.random.fold_in(rng, 6)
    for dim, shards_of in cuts:
        draws = jnp.exp(jax.random.uniform(jax.random.fold_in(own, dim), (shards_of,), jnp.float32, low / len(cuts), top_value / len(cuts)))
        loudness = loudness * jnp.repeat(draws, dims[dim] // shards_of).reshape([-1 if axis == dim else 1 for axis in range(len(dims))])
    return loudness


def centred(stream_key, dims, scale, most, shards=(), kind=jnp.bfloat16):
    values = jax.random.normal(stream_key, dims, jnp.float32) * scale
    if len(shards) > 0:
        values = level_of(stream_key, dims, shards, -0.22, 0.18) * values
    return jnp.clip(values, min=-most, max=most).astype(kind)


def setup_inputs(seed: int = 0, part: int = 0) -> dict:
    splits = jax.random.split(jax.random.key(seed), 10)
    part_splits = jax.random.split(jax.random.fold_in(splits[9], part), 10)
    queries = draw_queries(jax.random.fold_in(jax.random.fold_in(splits[9], part), 71), part)
    key_rows = draw_key_rows(jax.random.fold_in(jax.random.fold_in(splits[9], part), 71), part)
    values = centred(part_splits[2], (TOKENS, D_ATT), 1.0, 6.0, ((0, 8), (1, 2)))
    query_gain = jnp.clip(1.0 + 0.15 * jax.random.normal(splits[3], (D_ATT,), jnp.float32), 0.25, 1.75)
    key_gain = jnp.clip(1.0 + 0.15 * jax.random.normal(splits[4], (D_ATT,), jnp.float32), 0.25, 1.75)
    pattern = touch_ends((jax.random.randint(part_splits[5], (BLOCKS, 2 * WINDOW), 0, 5) < 3).astype(jnp.int32), jax.random.fold_in(part_splits[5], 1), 0, 1)
    reference_keys = centred(part_splits[6], (REF, D_ATT), 1.0, 6.0, ((0, 8), (1, 2)))
    reference_values = centred(part_splits[7], (REF, D_ATT), 1.0, 6.0, ((0, 8), (1, 2)))
    reference_live = touch_ends(jax.random.randint(part_splits[8], (BLOCKS,), 1, REF_DEV + 1), jax.random.fold_in(part_splits[8], 1), 1, REF_DEV).astype(jnp.int32)
    return dict(queries=queries, key_rows=key_rows, values=values, query_gain=query_gain, key_gain=key_gain, pattern=pattern, reference_keys=reference_keys, reference_values=reference_values, reference_live=reference_live)


EPSILON = 1e-06

def normalize(matrix, scaling):
    widened = matrix.astype(jnp.float32)
    mean_square = lax.optimization_barrier(jnp.mean(widened * widened, axis=1, keepdims=True))
    return (widened * lax.rsqrt(mean_square + EPSILON) * scaling).astype(jnp.bfloat16)

def offset_list():
    return [0] + [column - WINDOW for column in range(WINDOW)] + [column + 1 for column in range(WINDOW)]

def reference(queries, key_rows, values, query_gain, key_gain, pattern, reference_keys, reference_values, reference_live):
    scaling = HEAD_DIM ** (-0.5)
    normed_queries = normalize(queries, query_gain).reshape(BLOCKS, TOK_DEV, HEADS, HEAD_DIM)
    normed_keys = normalize(key_rows, key_gain).reshape(BLOCKS, TOK_DEV, HEADS, HEAD_DIM)
    value_blocks = values.reshape(BLOCKS, TOK_DEV, HEADS, HEAD_DIM)
    row_number = jnp.arange(REF, dtype=jnp.int32)
    live_rows = row_number % REF_DEV < jnp.repeat(reference_live, REF_DEV)
    extra_keys = reference_keys.reshape(REF, HEADS, HEAD_DIM).astype(jnp.float32)
    extra_values = reference_values.reshape(REF, HEADS, HEAD_DIM).astype(jnp.float32)
    shifts = jnp.array(offset_list(), dtype=jnp.int32)

    def one_block(block_id):
        chosen = (block_id + shifts) % BLOCKS
        near_keys = normed_keys[chosen].reshape(-1, HEADS, HEAD_DIM).astype(jnp.float32)
        near_values = value_blocks[chosen].reshape(-1, HEADS, HEAD_DIM).astype(jnp.float32)
        near_live = jnp.concatenate([jnp.ones((1,), jnp.int32), pattern[block_id].astype(jnp.int32)]) > 0
        allowed = jnp.concatenate([jnp.repeat(near_live, TOK_DEV), live_rows])
        all_keys = jnp.concatenate([near_keys, extra_keys], axis=0)
        all_values = jnp.concatenate([near_values, extra_values], axis=0)
        query_block = normed_queries[block_id].astype(jnp.float32)
        scores = jnp.einsum('thd,nhd->htn', query_block, all_keys, precision=lax.Precision.HIGHEST) * scaling
        scores = jnp.where(allowed[None, None, :], scores, -jnp.inf)
        row_peak = lax.optimization_barrier(jnp.max(scores, axis=2, keepdims=True))
        weights = jnp.exp(scores - row_peak)
        denominator = lax.optimization_barrier(jnp.sum(weights, axis=2))
        rounded = lax.optimization_barrier(weights.astype(jnp.bfloat16)).astype(jnp.float32)
        summed = jnp.einsum('htn,nhd->thd', rounded, all_values, precision=lax.Precision.HIGHEST)
        return (summed / jnp.transpose(denominator)[:, :, None]).astype(jnp.bfloat16)
    result = lax.map(one_block, jnp.arange(BLOCKS, dtype=jnp.int32))
    return result.reshape(TOKENS, HEADS * HEAD_DIM)
```

```python
import functools
import math

import jax
import jax.numpy as jnp
from jax import lax
from jax.experimental import pallas as pl
from jax.experimental.pallas import tpu as pltpu
from jax.sharding import PartitionSpec as P

HEADS = 20
HEAD_DIM = 128
WINDOW = 2
EPSILON = 1e-06
LANES = 128
TO_LOG2 = HEAD_DIM ** (-0.5) * math.log2(math.e)


def fetch(block, source_of):
    n = lax.axis_size("frm")
    return lax.ppermute(block, "frm", [(source_of(i) % n, i) for i in range(n)])


def after(value, *earlier):
    return lax.optimization_barrier((value,) + earlier)[0]


def far_first(i):
    return i + WINDOW if i % 2 == 0 else i - WINDOW


def far_second(i):
    return i - WINDOW if i % 2 == 0 else i + WINDOW


def beside(i):
    return i + 1 if i % 2 == 0 else i - 1


def gather_rows(rows):
    n = lax.axis_size("frm")
    if n & (n - 1):
        return lax.all_gather(rows, "frm", axis=0, tiled=True)
    distance = 1
    while distance < n:
        rows = jnp.concatenate([rows, fetch(rows, lambda i: i ^ distance)], axis=0)
        distance *= 2
    return rows


def attend_kernel(blocks, has_state, last, *refs):
    refs = list(refs)
    query_ref, bias_ref = refs[:2]
    key_refs = refs[2 : 2 + blocks]
    value_refs = refs[2 + blocks : 2 + 2 * blocks]
    rest = refs[2 + 2 * blocks :]
    if has_state:
        old_stats_ref, old_total_ref = rest[:2]
        rest = rest[2:]
    tokens, features = query_ref.shape
    heads = features // HEAD_DIM
    bias = bias_ref[...]
    lane = lax.broadcasted_iota(jnp.int32, (tokens, LANES), 1)
    stats = jnp.zeros((tokens, LANES), jnp.float32)
    for head in range(heads):
        columns = pl.ds(head * HEAD_DIM, HEAD_DIM)
        keys = jnp.concatenate([ref[:, columns] for ref in key_refs], axis=0)
        values = jnp.concatenate([ref[:, columns] for ref in value_refs], axis=0)
        scores = lax.dot_general(
            query_ref[:, columns],
            keys,
            (((1,), (1,)), ((), ())),
            preferred_element_type=jnp.float32,
        )
        scores = scores * TO_LOG2 + bias
        peak = jnp.max(scores, axis=1, keepdims=True)
        if has_state:
            old_peak = old_stats_ref[:, head : head + 1]
            peak = jnp.maximum(peak, old_peak)
        weights = jnp.exp2(scores - peak)
        total = jnp.sum(weights, axis=1, keepdims=True)
        numerator = jnp.dot(
            weights.astype(jnp.bfloat16), values, preferred_element_type=jnp.float32
        )
        if has_state:
            fading = jnp.exp2(old_peak - peak)
            total = total + old_stats_ref[:, heads + head : heads + head + 1] * fading
            numerator = numerator + old_total_ref[:, columns] * fading
        if last:
            rest[0][:, columns] = (numerator / total).astype(jnp.bfloat16)
        else:
            rest[1][:, columns] = numerator
            stats = jnp.where(lane == head, peak, stats)
            stats = jnp.where(lane == heads + head, total, stats)
    if not last:
        rest[0][...] = stats


def attend(queries, bias, keys, values, state=(), last=False):
    tokens, features = queries.shape
    rows = bias.shape[1]
    if last:
        out_shape = jax.ShapeDtypeStruct((tokens, features), jnp.bfloat16)
    else:
        out_shape = (
            jax.ShapeDtypeStruct((tokens, LANES), jnp.float32),
            jax.ShapeDtypeStruct((tokens, features), jnp.float32),
        )
    heads = features // HEAD_DIM
    return pl.pallas_call(
        functools.partial(attend_kernel, len(keys), bool(state), last),
        out_shape=out_shape,
        cost_estimate=pl.CostEstimate(
            flops=4 * tokens * rows * features,
            transcendentals=heads * tokens * rows,
            bytes_accessed=4 * rows * features + 4 * tokens * features,
        ),
        name="attend_last" if last else "attend",
    )(queries, bias, *keys, *values, *state)


def shards(
    queries,
    key_rows,
    values,
    query_gain,
    key_gain,
    pattern,
    reference_keys,
    reference_values,
    reference_live,
):
    tokens, features = queries.shape
    heads = features // HEAD_DIM
    even = lax.axis_index("frm") % 2 == 0

    far1_values = fetch(values, far_first)
    near_values = fetch(values, beside)

    slots = reference_keys.shape[0]
    live = (jnp.arange(slots, dtype=jnp.int32) < reference_live[0]).astype(jnp.bfloat16)
    reference_rows = jnp.concatenate(
        [
            reference_keys,
            reference_values,
            jnp.broadcast_to(live[:, None], (slots, LANES)),
        ],
        axis=1,
    )
    reference_rows = gather_rows(reference_rows)

    squares = lax.psum(
        jnp.stack(
            [
                jnp.sum(jnp.square(rows.astype(jnp.float32)), axis=1)
                for rows in (queries, key_rows)
            ]
        ),
        "tp",
    )

    def normalize(rows, gain, square_sum):
        scale = lax.rsqrt(square_sum / (HEADS * HEAD_DIM) + EPSILON)
        return (rows.astype(jnp.float32) * scale[:, None] * gain).astype(jnp.bfloat16)

    normed_keys = normalize(key_rows, key_gain, squares[1])
    normed_queries = normalize(queries, query_gain, squares[0])

    far1_keys = fetch(normed_keys, far_first)
    near_keys = fetch(normed_keys, beside)
    far2_values = fetch(after(values, far1_values), far_second)
    passed_values = fetch(far1_values, beside)
    far2_keys = fetch(after(normed_keys, far1_keys), far_second)
    passed_keys = fetch(far1_keys, beside)

    flags = jnp.where(even, pattern[0, ::-1], pattern[0]) > 0
    closed = jnp.where(flags, 0.0, -jnp.inf).astype(jnp.float32)
    spread = jnp.repeat(closed, tokens)[None, :]
    far1_bias, near_bias, passed_bias, far2_bias = (
        spread[:, i * tokens : (i + 1) * tokens] for i in range(4)
    )
    own_bias = jnp.zeros((1, tokens), jnp.float32)
    reference_bias = jnp.where(
        reference_rows[:, 2 * features] > 0.5, 0.0, -jnp.inf
    ).astype(jnp.float32)[None, :]

    state = attend(
        normed_queries,
        jnp.concatenate([own_bias, near_bias], axis=1),
        [normed_keys, near_keys],
        [values, near_values],
    )
    state = attend(
        normed_queries,
        jnp.concatenate([far1_bias, reference_bias], axis=1),
        [far1_keys, reference_rows[:, :features]],
        [far1_values, reference_rows[:, features : 2 * features]],
        state,
    )
    return attend(
        normed_queries,
        jnp.concatenate([passed_bias, far2_bias], axis=1),
        [passed_keys, far2_keys],
        [passed_values, far2_values],
        state,
        last=True,
    )


def solution(mesh):
    in_specs = (
        P(("grp", "frm"), "tp"),
        P(("grp", "frm"), "tp"),
        P(("grp", "frm"), "tp"),
        P("tp"),
        P("tp"),
        P(("grp", "frm"), None),
        P(("grp", "frm"), "tp"),
        P(("grp", "frm"), "tp"),
        P(("grp", "frm")),
    )
    out_specs = P(("grp", "frm"), "tp")
    return jax.shard_map(shards, mesh=mesh, in_specs=in_specs, out_specs=out_specs, check_vma=False)
```

```python
import math

import jax
import jax.numpy as jnp
from jax import lax
from jax.experimental import pallas as pl
from jax.experimental.pallas import tpu as pltpu
from jax.sharding import PartitionSpec as P

HEADS = 20
HEAD_DIM = 128
WINDOW = 2
EPSILON = 1e-06
LANES = 128
SCRATCH_BYTES = 24 * 2**20
DEAD = 100.0
TO_LOG2 = HEAD_DIM ** (-0.5) * math.log2(math.e)


def fetch(block, source_of, axis="frm"):
    n = lax.axis_size(axis)
    return lax.ppermute(block, axis, [(source_of(i) % n, i) for i in range(n)])


def after(value, *earlier):
    return lax.optimization_barrier((value,) + earlier)[0]


def far_first(i):
    return i + WINDOW if i % 2 == 0 else i - WINDOW


def far_second(i):
    return i - WINDOW if i % 2 == 0 else i + WINDOW


def beside(i):
    return i + 1 if i % 2 == 0 else i - 1


def in_vmem(array):
    return pltpu.with_memory_space_constraint(array, pltpu.VMEM)


VMEM = pl.BlockSpec(memory_space=pltpu.VMEM)
SMEM = pl.BlockSpec(memory_space=pltpu.SMEM)
PARAMS = pltpu.CompilerParams(vmem_limit_bytes=SCRATCH_BYTES)


CHEAP = pl.CostEstimate(flops=1, transcendentals=0, bytes_accessed=1)


def head_columns(head):
    return slice(head * HEAD_DIM, (head + 1) * HEAD_DIM)


def score(queries, keys):
    return lax.dot_general(
        queries, keys, (((1,), (1,)), ((), ())), preferred_element_type=jnp.float32
    )


def pack_kernel(live_ref, keys_ref, values_ref, rows_ref, live_smem, sems):
    slots, features = keys_ref.shape
    copies = [
        pltpu.make_async_copy(live_ref, live_smem, sems.at[0]),
        pltpu.make_async_copy(keys_ref, rows_ref.at[:, :features], sems.at[1]),
        pltpu.make_async_copy(values_ref, rows_ref.at[:, features:], sems.at[2]),
    ]
    for copy in copies:
        copy.start()
    for copy in copies:
        copy.wait()
    slot = lax.broadcasted_iota(jnp.int32, (slots, features), 0)
    keys = rows_ref[:, :features].astype(jnp.float32)
    rows_ref[:, :features] = jnp.where(slot < live_smem[0], keys, DEAD).astype(jnp.bfloat16)


def pack_rows(live, keys, values):
    slots, features = keys.shape
    return pl.pallas_call(
        pack_kernel,
        out_shape=pltpu.VMEM((slots, 2 * features), jnp.bfloat16),
        in_specs=[pl.BlockSpec(memory_space=pl.ANY)] * 3,
        out_specs=VMEM,
        scratch_shapes=[pltpu.SMEM((1,), jnp.int32), pltpu.SemaphoreType.DMA((3,))],
        compiler_params=PARAMS,
        cost_estimate=CHEAP,
        name="pack_rows",
    )(live, keys, values)


def attach_kernel(keys_ref, *refs):
    *row_refs, packed_ref = refs
    tokens, features = keys_ref.shape
    packed_ref[:tokens] = keys_ref[...]
    count = sum(ref.shape[0] for ref in row_refs)
    first = tokens
    for ref in row_refs:
        slots = ref.shape[0]
        packed_ref[first : first + slots] = ref[:, :features]
        packed_ref[first + count : first + count + slots] = ref[:, features:]
        first += slots


def attach_rows(keys, rows):
    tokens, features = keys.shape
    count = sum(part.shape[0] for part in rows)
    return pl.pallas_call(
        attach_kernel,
        out_shape=pltpu.VMEM((tokens + 2 * count, features), jnp.bfloat16),
        in_specs=[VMEM] * (1 + len(rows)),
        out_specs=VMEM,
        compiler_params=PARAMS,
        cost_estimate=CHEAP,
        name="attach_rows",
    )(*map(in_vmem, (keys, *rows)))


def squares_kernel(first_ref, second_ref, squares_ref):
    def square_sum(ref):
        rows = ref[: squares_ref.shape[0]].astype(jnp.float32)
        return jnp.sum(rows * rows, axis=1, keepdims=True)

    lane = lax.broadcasted_iota(jnp.int32, squares_ref.shape, 1)
    squares_ref[...] = jnp.where(lane == 0, square_sum(first_ref), square_sum(second_ref))


def square_sums(first, second, name):
    squares = pl.pallas_call(
        squares_kernel,
        out_shape=pltpu.VMEM((min(first.shape[0], second.shape[0]), LANES), jnp.float32),
        in_specs=[VMEM, VMEM],
        out_specs=VMEM,
        compiler_params=PARAMS,
        cost_estimate=CHEAP,
        name=name,
    )(in_vmem(first), in_vmem(second))
    return squares, fetch(squares, lambda i: i ^ 1, "tp")


def normalized(rows_ref, gain_ref, squares_refs, column):
    square_sum = sum(ref[:, column : column + 1] for ref in squares_refs)
    scale = lax.rsqrt(square_sum / (HEADS * HEAD_DIM) + EPSILON)
    rows = rows_ref[: square_sum.shape[0]].astype(jnp.float32)
    return (rows * scale * gain_ref[...][None, :]).astype(jnp.bfloat16)


def pattern_flag(pattern_ref, column):
    even = lax.rem(lax.axis_index("frm"), 2) == 0
    return jnp.where(even, pattern_ref[0, 2 * WINDOW - 1 - column], pattern_ref[0, column]) > 0


def block_bias(flag, tokens):
    return jnp.where(flag, jnp.zeros((1, tokens), jnp.float32), -jnp.inf)


def early_kernel(
    pattern_ref,
    query_gain,
    key_gain,
    queries,
    own_keys,
    near_keys,
    far_keys,
    own_squares,
    other_own_squares,
    far_squares,
    other_far_squares,
    own_values,
    near_values,
    far_values,
    query_ref,
    peaks_ref,
    totals_ref,
    partial_ref,
    keys_ref,
    scores_ref,
    weights_ref,
):
    tokens, features = query_ref.shape
    heads = features // HEAD_DIM
    bias = jnp.concatenate(
        [
            jnp.zeros((1, tokens), jnp.float32),
            block_bias(pattern_flag(pattern_ref, 1), tokens),
            block_bias(pattern_flag(pattern_ref, 0), tokens),
        ],
        axis=1,
    )
    own, far = (own_squares, other_own_squares), (far_squares, other_far_squares)
    query_ref[...] = normalized(queries, query_gain, own, 0)
    keys_ref[:tokens] = normalized(own_keys, key_gain, own, 1)
    keys_ref[tokens : 2 * tokens] = normalized(near_keys, key_gain, far, 0)
    keys_ref[2 * tokens :] = normalized(far_keys, key_gain, far, 1)
    for head in range(heads):
        columns = head_columns(head)
        scores_ref[head] = score(query_ref[:, columns], keys_ref[:, columns])
    for head in range(heads):
        scores = scores_ref[head] * TO_LOG2 + bias
        peak = jnp.max(scores, axis=1, keepdims=True)
        weights = jnp.exp2(scores - peak)
        total = jnp.sum(weights, axis=1, keepdims=True)
        weights_ref[head] = weights.astype(jnp.bfloat16)
        peaks_ref[head] = jnp.broadcast_to(peak, (tokens, LANES))
        totals_ref[head] = jnp.broadcast_to(total, (tokens, LANES))
    for head in range(heads):
        columns = head_columns(head)
        values = [ref[:, columns] for ref in (own_values, near_values, far_values)]
        partial_ref[:, columns] = jnp.dot(
            weights_ref[head],
            jnp.concatenate(values, axis=0),
            preferred_element_type=jnp.float32,
        )


def late_keys_kernel(
    pattern_ref,
    key_gain,
    query_ref,
    passed_keys,
    far_keys,
    squares,
    other_squares,
    own_packed,
    near_packed,
    old_peaks_ref,
    old_totals_ref,
    old_partial_ref,
    inverses_ref,
    partial_ref,
    weights_ref,
    keys_ref,
    values_ref,
    scores_ref,
):
    tokens, features = query_ref.shape
    heads = features // HEAD_DIM
    blocks = 2 * tokens
    count = values_ref.shape[0] // 2
    for place, packed in enumerate((own_packed, near_packed)):
        first = place * count
        keys_ref[blocks + first : blocks + first + count] = packed[tokens : tokens + count]
        values_ref[first : first + count] = packed[tokens + count :]
    marks = score(jnp.ones((8, LANES), jnp.bfloat16), keys_ref[blocks:, :LANES])
    bias = jnp.concatenate(
        [
            block_bias(pattern_flag(pattern_ref, 2), tokens),
            block_bias(pattern_flag(pattern_ref, 3), tokens),
            jnp.where(marks[:1] < 0.5 * DEAD * LANES, 0.0, -jnp.inf),
        ],
        axis=1,
    )
    keys_ref[:tokens] = normalized(passed_keys, key_gain, (squares, other_squares), 0)
    keys_ref[tokens:blocks] = normalized(far_keys, key_gain, (squares, other_squares), 1)
    for head in range(heads):
        columns = head_columns(head)
        scores_ref[head] = score(query_ref[:, columns], keys_ref[:, columns])
    for head in range(heads):
        columns = head_columns(head)
        scores = scores_ref[head] * TO_LOG2 + bias
        old_peak = old_peaks_ref[head]
        peak = jnp.maximum(old_peak, jnp.max(scores, axis=1, keepdims=True))
        weights = jnp.exp2(scores - peak[:, :1])
        total = jnp.sum(weights, axis=1, keepdims=True)
        weights = weights.astype(jnp.bfloat16)
        fading = jnp.exp2(old_peak - peak)
        inverse = 1.0 / (old_totals_ref[head] * fading + total)
        inverses_ref[head] = inverse
        weights_ref[head] = weights[:, :blocks]
        product = jnp.dot(
            weights[:, blocks:],
            values_ref[:, columns],
            preferred_element_type=jnp.float32,
        )
        partial_ref[:, columns] = (old_partial_ref[:, columns] * fading + product) * inverse


def late_values_kernel(
    inverses_ref, partial_ref, weights_ref, passed_values, far_values, out_ref, out_vmem, sems
):
    heads = weights_ref.shape[0]
    copies = []
    for head in range(heads):
        columns = head_columns(head)
        values = jnp.concatenate([passed_values[:, columns], far_values[:, columns]], axis=0)
        product = jnp.dot(weights_ref[head], values, preferred_element_type=jnp.float32)
        out_vmem[:, columns] = (
            partial_ref[:, columns] + product * inverses_ref[head]
        ).astype(jnp.bfloat16)
        copy = pltpu.make_async_copy(
            out_vmem.at[:, columns], out_ref.at[:, columns], sems.at[head]
        )
        copy.start()
        copies.append(copy)
    for copy in copies:
        copy.wait()


def attend_early(pattern, gains, queries, keys, squares, values):
    tokens, features = queries.shape
    heads = features // HEAD_DIM
    count = 3 * tokens
    return pl.pallas_call(
        early_kernel,
        out_shape=(
            pltpu.VMEM((tokens, features), jnp.bfloat16),
            pltpu.VMEM((heads, tokens, LANES), jnp.float32),
            pltpu.VMEM((heads, tokens, LANES), jnp.float32),
            pltpu.VMEM((tokens, features), jnp.float32),
        ),
        in_specs=[SMEM] + [VMEM] * 13,
        out_specs=(VMEM,) * 4,
        scratch_shapes=[
            pltpu.VMEM((count, features), jnp.bfloat16),
            pltpu.VMEM((heads, tokens, count), jnp.float32),
            pltpu.VMEM((heads, tokens, count), jnp.bfloat16),
        ],
        compiler_params=PARAMS,
        cost_estimate=CHEAP,
        name="attend_early",
    )(pattern, *map(in_vmem, (*gains, queries, *keys, *squares, *values)))


def attend_late_keys(pattern, gain, queries, keys, squares, packed, early):
    tokens, features = queries.shape
    heads = features // HEAD_DIM
    rows = packed[0].shape[0] - tokens
    count = 2 * tokens + rows
    return pl.pallas_call(
        late_keys_kernel,
        out_shape=(
            pltpu.VMEM((heads, tokens, LANES), jnp.float32),
            pltpu.VMEM((tokens, features), jnp.float32),
            pltpu.VMEM((heads, tokens, 2 * tokens), jnp.bfloat16),
        ),
        in_specs=[SMEM] + [VMEM] * 11,
        out_specs=(VMEM,) * 3,
        scratch_shapes=[
            pltpu.VMEM((count, features), jnp.bfloat16),
            pltpu.VMEM((rows, features), jnp.bfloat16),
            pltpu.VMEM((heads, tokens, count), jnp.float32),
        ],
        compiler_params=PARAMS,
        cost_estimate=CHEAP,
        name="attend_late_keys",
    )(pattern, *map(in_vmem, (gain, queries, *keys, *squares, *packed, *early)))


def attend_late_values(inverses, partial, weights, values):
    tokens, features = partial.shape
    heads = features // HEAD_DIM
    return pl.pallas_call(
        late_values_kernel,
        out_shape=jax.ShapeDtypeStruct((tokens, features), jnp.bfloat16),
        in_specs=[VMEM] * 5,
        out_specs=pl.BlockSpec(memory_space=pl.ANY),
        scratch_shapes=[
            pltpu.VMEM((tokens, features), jnp.bfloat16),
            pltpu.SemaphoreType.DMA((heads,)),
        ],
        compiler_params=PARAMS,
        cost_estimate=CHEAP,
        name="attend_late_values",
    )(*map(in_vmem, (inverses, partial, weights, *values)))


def column_rows(rows):
    n = lax.axis_size("frm")
    if n <= 8:
        return [rows] + [fetch(rows, lambda i: i + distance) for distance in range(2, n, 2)]
    distance = n // 2
    while distance > 1:
        rows = jnp.concatenate([rows, fetch(rows, lambda i: i ^ distance)], axis=0)
        distance //= 2
    return [rows]


def shards(
    queries,
    key_rows,
    values,
    query_gain,
    key_gain,
    pattern,
    reference_keys,
    reference_values,
    reference_live,
):
    rows = column_rows(pack_rows(reference_live, reference_keys, reference_values))
    packed_keys = attach_rows(key_rows, rows)

    far1_keys = fetch(key_rows, far_first)
    near_values = fetch(values, beside)
    far1_values = fetch(values, far_first)
    near_packed = fetch(packed_keys, beside)
    far2_keys = fetch(key_rows, far_second)
    far2_values = fetch(values, far_second)
    passed_keys = fetch(far1_keys, beside)
    passed_values = fetch(far1_values, beside)

    own_squares = square_sums(queries, packed_keys, "own_squares")
    far_squares = square_sums(near_packed, far1_keys, "early_squares")
    normed_queries, *early = attend_early(
        pattern,
        (query_gain, key_gain),
        queries,
        (packed_keys, near_packed, far1_keys),
        (*own_squares, *far_squares),
        (values, near_values, far1_values),
    )
    passed_keys = after(passed_keys, early[0])
    late_squares = square_sums(passed_keys, far2_keys, "late_squares")
    inverses, partial, weights = attend_late_keys(
        pattern,
        key_gain,
        normed_queries,
        (passed_keys, far2_keys),
        late_squares,
        (packed_keys, near_packed),
        early,
    )
    return attend_late_values(inverses, partial, weights, (passed_values, far2_values))


def solution(mesh):
    in_specs = (
        P(("grp", "frm"), "tp"),
        P(("grp", "frm"), "tp"),
        P(("grp", "frm"), "tp"),
        P("tp"),
        P("tp"),
        P(("grp", "frm"), None),
        P(("grp", "frm"), "tp"),
        P(("grp", "frm"), "tp"),
        P(("grp", "frm")),
    )
    out_specs = P(("grp", "frm"), "tp")
    return jax.shard_map(shards, mesh=mesh, in_specs=in_specs, out_specs=out_specs, check_vma=False)
```

```python
import math

import jax
import jax.numpy as jnp
from jax import lax
from jax.experimental import pallas as pl
from jax.experimental.pallas import tpu as pltpu
from jax.sharding import PartitionSpec as P

HEADS = 20
HEAD_DIM = 128
WINDOW = 2
EPSILON = 1e-06
LANES = 128
SCRATCH_BYTES = 24 * 2**20
DEAD = 100.0
TO_LOG2 = HEAD_DIM ** (-0.5) * math.log2(math.e)


def fetch(block, source_of, axis="frm"):
    n = lax.axis_size(axis)
    return lax.ppermute(block, axis, [(source_of(i) % n, i) for i in range(n)])


def after(value, *earlier):
    return lax.optimization_barrier((value,) + earlier)[0]


def far_first(i):
    return i + WINDOW if i % 2 == 0 else i - WINDOW


def far_second(i):
    return i - WINDOW if i % 2 == 0 else i + WINDOW


def beside(i):
    return i + 1 if i % 2 == 0 else i - 1


def in_vmem(array):
    return pltpu.with_memory_space_constraint(array, pltpu.VMEM)


def in_hbm(array):
    return pltpu.with_memory_space_constraint(array, pltpu.HBM)


VMEM = pl.BlockSpec(memory_space=pltpu.VMEM)
SMEM = pl.BlockSpec(memory_space=pltpu.SMEM)
PARAMS = pltpu.CompilerParams(vmem_limit_bytes=SCRATCH_BYTES)


CHEAP = pl.CostEstimate(flops=1, transcendentals=0, bytes_accessed=1)


def head_columns(head):
    return slice(head * HEAD_DIM, (head + 1) * HEAD_DIM)


def score(queries, keys):
    return lax.dot_general(
        queries, keys, (((1,), (1,)), ((), ())), preferred_element_type=jnp.float32
    )


def pack_kernel(live_ref, keys_ref, values_ref, rows_ref, live_smem, sems):
    slots, features = keys_ref.shape
    copies = [
        pltpu.make_async_copy(live_ref, live_smem, sems.at[0]),
        pltpu.make_async_copy(keys_ref, rows_ref.at[:, :features], sems.at[1]),
        pltpu.make_async_copy(values_ref, rows_ref.at[:, features:], sems.at[2]),
    ]
    for copy in copies:
        copy.start()
    for copy in copies:
        copy.wait()
    slot = lax.broadcasted_iota(jnp.int32, (slots, features), 0)
    keys = rows_ref[:, :features].astype(jnp.float32)
    rows_ref[:, :features] = jnp.where(slot < live_smem[0], keys, DEAD).astype(jnp.bfloat16)


def pack_rows(live, keys, values):
    slots, features = keys.shape
    return pl.pallas_call(
        pack_kernel,
        out_shape=pltpu.VMEM((slots, 2 * features), jnp.bfloat16),
        in_specs=[pl.BlockSpec(memory_space=pltpu.HBM)] * 3,
        out_specs=VMEM,
        scratch_shapes=[pltpu.SMEM((1,), jnp.int32), pltpu.SemaphoreType.DMA((3,))],
        compiler_params=PARAMS,
        cost_estimate=CHEAP,
        name="pack_rows",
    )(live, in_hbm(keys), in_hbm(values))


def squares_kernel(*refs):
    *row_refs, squares_ref = refs
    lane = lax.broadcasted_iota(jnp.int32, squares_ref.shape, 1)
    squares = jnp.zeros(squares_ref.shape, jnp.float32)
    for column, ref in enumerate(row_refs):
        rows = ref[...].astype(jnp.float32)
        squares = jnp.where(lane == column, jnp.sum(rows * rows, axis=1, keepdims=True), squares)
    squares_ref[...] = squares


def square_sums(name, blocks, earlier=()):
    squares = pl.pallas_call(
        squares_kernel,
        out_shape=pltpu.VMEM((blocks[0].shape[0], LANES), jnp.float32),
        in_specs=[VMEM] * len(blocks),
        out_specs=VMEM,
        compiler_params=PARAMS,
        cost_estimate=CHEAP,
        name=name,
    )(*map(in_vmem, blocks))
    squares = after(squares, *earlier)
    return squares, fetch(squares, lambda i: i ^ 1, "tp")


def normalized(rows_ref, gain_ref, squares_refs, column):
    square_sum = sum(ref[:, column : column + 1] for ref in squares_refs)
    scale = lax.rsqrt(square_sum / (HEADS * HEAD_DIM) + EPSILON)
    rows = rows_ref[...].astype(jnp.float32)
    return (rows * scale * gain_ref[...][None, :]).astype(jnp.bfloat16)


def prepare_kernel(
    queries, keys, query_gain, key_gain, squares, other_squares, query_ref, key_ref
):
    query_ref[...] = normalized(queries, query_gain, (squares, other_squares), 0)
    key_ref[...] = normalized(keys, key_gain, (squares, other_squares), 1)


def prepare(queries, keys, gains, squares):
    return pl.pallas_call(
        prepare_kernel,
        out_shape=(pltpu.VMEM(keys.shape, jnp.bfloat16),) * 2,
        in_specs=[VMEM] * 6,
        out_specs=(VMEM,) * 2,
        compiler_params=PARAMS,
        cost_estimate=CHEAP,
        name="prepare",
    )(*map(in_vmem, (queries, keys, *gains, *squares)))


def prepare_far_kernel(keys, gain, squares, other_squares, *refs):
    *row_refs, packed_ref = refs
    tokens, features = keys.shape
    count = (packed_ref.shape[0] - tokens) // 2
    packed_ref[:tokens] = normalized(keys, gain, (squares, other_squares), 0)
    first = tokens
    for ref in row_refs:
        slots = ref.shape[0]
        packed_ref[first : first + slots] = ref[:, :features]
        packed_ref[first + count : first + count + slots] = ref[:, features:]
        first += slots


def prepare_far(keys, gain, squares, rows):
    tokens, features = keys.shape
    count = sum(part.shape[0] for part in rows)
    return pl.pallas_call(
        prepare_far_kernel,
        out_shape=pltpu.VMEM((tokens + 2 * count, features), jnp.bfloat16),
        in_specs=[VMEM] * (4 + len(rows)),
        out_specs=VMEM,
        compiler_params=PARAMS,
        cost_estimate=CHEAP,
        name="prepare_far",
    )(*map(in_vmem, (keys, gain, *squares, *rows)))


def pattern_flag(pattern_ref, column):
    even = lax.rem(lax.axis_index("frm"), 2) == 0
    return jnp.where(even, pattern_ref[0, 2 * WINDOW - 1 - column], pattern_ref[0, column]) > 0


def block_bias(flag, tokens):
    return jnp.where(flag, jnp.zeros((1, tokens), jnp.float32), -jnp.inf)


def softmax_parts(scores_ref, head, bias):
    scores = scores_ref[head] * TO_LOG2 + bias
    return scores, jnp.max(scores, axis=1, keepdims=True)


def early_kernel(
    pattern_ref,
    query_ref,
    own_keys,
    near_keys,
    far_packed,
    own_values,
    near_values,
    far_values,
    peaks_ref,
    totals_ref,
    partial_ref,
    scores_ref,
    weights_ref,
):
    tokens, features = query_ref.shape
    heads = features // HEAD_DIM
    bias = jnp.concatenate(
        [
            jnp.zeros((1, tokens), jnp.float32),
            block_bias(pattern_flag(pattern_ref, 1), tokens),
            block_bias(pattern_flag(pattern_ref, 0), tokens),
        ],
        axis=1,
    )
    for head in range(heads):
        columns = head_columns(head)
        keys = [own_keys[:, columns], near_keys[:, columns], far_packed[:tokens, columns]]
        scores_ref[head] = score(query_ref[:, columns], jnp.concatenate(keys, axis=0))
    for head in range(heads):
        scores, peak = softmax_parts(scores_ref, head, bias)
        weights = jnp.exp2(scores - peak)
        total = jnp.sum(weights, axis=1, keepdims=True)
        weights_ref[head] = weights.astype(jnp.bfloat16)
        peaks_ref[head] = jnp.broadcast_to(peak, (tokens, LANES))
        totals_ref[head] = jnp.broadcast_to(total, (tokens, LANES))
    for head in range(heads):
        columns = head_columns(head)
        values = [ref[:, columns] for ref in (own_values, near_values, far_values)]
        partial_ref[:, columns] = jnp.dot(
            weights_ref[head],
            jnp.concatenate(values, axis=0),
            preferred_element_type=jnp.float32,
        )


def late_keys_kernel(
    pattern_ref,
    query_ref,
    own_packed,
    passed_packed,
    far_keys,
    old_peaks_ref,
    old_totals_ref,
    old_partial_ref,
    inverses_ref,
    partial_ref,
    weights_ref,
    keys_ref,
    values_ref,
    scores_ref,
):
    tokens, features = query_ref.shape
    heads = features // HEAD_DIM
    blocks = 2 * tokens
    count = values_ref.shape[0] // 2
    keys_ref[:tokens] = passed_packed[:tokens]
    keys_ref[tokens:blocks] = far_keys[...]
    for place, packed in enumerate((own_packed, passed_packed)):
        first = place * count
        keys_ref[blocks + first : blocks + first + count] = packed[tokens : tokens + count]
        values_ref[first : first + count] = packed[tokens + count :]
    marks = score(jnp.ones((8, LANES), jnp.bfloat16), keys_ref[blocks:, :LANES])
    bias = jnp.concatenate(
        [
            block_bias(pattern_flag(pattern_ref, 2), tokens),
            block_bias(pattern_flag(pattern_ref, 3), tokens),
            jnp.where(marks[:1] < 0.5 * DEAD * LANES, 0.0, -jnp.inf),
        ],
        axis=1,
    )
    for head in range(heads):
        columns = head_columns(head)
        scores_ref[head] = score(query_ref[:, columns], keys_ref[:, columns])
    for head in range(heads):
        columns = head_columns(head)
        scores, peak = softmax_parts(scores_ref, head, bias)
        old_peak = old_peaks_ref[head]
        peak = jnp.maximum(old_peak, peak)
        weights = jnp.exp2(scores - peak[:, :1])
        fading = jnp.exp2(old_peak - peak)
        total = jnp.sum(weights, axis=1, keepdims=True)
        inverse = 1.0 / (old_totals_ref[head] * fading + total)
        inverses_ref[head] = inverse
        weights = weights.astype(jnp.bfloat16)
        weights_ref[head] = weights[:, :blocks]
        product = jnp.dot(
            weights[:, blocks:], values_ref[:, columns], preferred_element_type=jnp.float32
        )
        partial_ref[:, columns] = (old_partial_ref[:, columns] * fading + product) * inverse


def late_values_kernel(
    inverses_ref, partial_ref, weights_ref, passed_values, far_values, out_ref, out_vmem, sems
):
    heads = weights_ref.shape[0]
    copies = []
    for head in range(heads):
        columns = head_columns(head)
        values = jnp.concatenate([passed_values[:, columns], far_values[:, columns]], axis=0)
        product = jnp.dot(weights_ref[head], values, preferred_element_type=jnp.float32)
        out_vmem[:, columns] = (
            partial_ref[:, columns] + product * inverses_ref[head]
        ).astype(jnp.bfloat16)
        copy = pltpu.make_async_copy(
            out_vmem.at[:, columns], out_ref.at[:, columns], sems.at[head]
        )
        copy.start()
        copies.append(copy)
    for copy in copies:
        copy.wait()


def attend_early(pattern, queries, keys, values):
    tokens, features = queries.shape
    heads = features // HEAD_DIM
    count = 3 * tokens
    return pl.pallas_call(
        early_kernel,
        out_shape=(
            pltpu.VMEM((heads, tokens, LANES), jnp.float32),
            pltpu.VMEM((heads, tokens, LANES), jnp.float32),
            pltpu.VMEM((tokens, features), jnp.float32),
        ),
        in_specs=[SMEM] + [VMEM] * 7,
        out_specs=(VMEM,) * 3,
        scratch_shapes=[
            pltpu.VMEM((heads, tokens, count), jnp.float32),
            pltpu.VMEM((heads, tokens, count), jnp.bfloat16),
        ],
        compiler_params=PARAMS,
        cost_estimate=CHEAP,
        name="attend_early",
    )(pattern, *map(in_vmem, (queries, *keys, *values)))


def attend_late_keys(pattern, queries, own_packed, passed_packed, far_keys, state):
    tokens, features = queries.shape
    heads = features // HEAD_DIM
    rows = own_packed.shape[0] - tokens
    count = 2 * tokens + rows
    return pl.pallas_call(
        late_keys_kernel,
        out_shape=(
            pltpu.VMEM((heads, tokens, LANES), jnp.float32),
            pltpu.VMEM((tokens, features), jnp.float32),
            pltpu.VMEM((heads, tokens, 2 * tokens), jnp.bfloat16),
        ),
        in_specs=[SMEM] + [VMEM] * 7,
        out_specs=(VMEM,) * 3,
        scratch_shapes=[
            pltpu.VMEM((count, features), jnp.bfloat16),
            pltpu.VMEM((rows, features), jnp.bfloat16),
            pltpu.VMEM((heads, tokens, count), jnp.float32),
        ],
        compiler_params=PARAMS,
        cost_estimate=CHEAP,
        name="attend_late_keys",
    )(pattern, *map(in_vmem, (queries, own_packed, passed_packed, far_keys, *state)))


def attend_late_values(inverses, partial, weights, values):
    tokens, features = partial.shape
    heads = features // HEAD_DIM
    return pl.pallas_call(
        late_values_kernel,
        out_shape=jax.ShapeDtypeStruct((tokens, features), jnp.bfloat16),
        in_specs=[VMEM] * 5,
        out_specs=pl.BlockSpec(memory_space=pl.ANY),
        scratch_shapes=[
            pltpu.VMEM((tokens, features), jnp.bfloat16),
            pltpu.SemaphoreType.DMA((heads,)),
        ],
        compiler_params=PARAMS,
        cost_estimate=CHEAP,
        name="attend_late_values",
    )(*map(in_vmem, (inverses, partial, weights, *values)))


def column_rows(rows):
    n = lax.axis_size("frm")
    if n <= 8:
        return [rows] + [fetch(rows, lambda i: i + distance) for distance in range(2, n, 2)]
    distance = n // 2
    while distance > 1:
        rows = jnp.concatenate([rows, fetch(rows, lambda i: i ^ distance)], axis=0)
        distance //= 2
    return [rows]


def shards(
    queries,
    key_rows,
    values,
    query_gain,
    key_gain,
    pattern,
    reference_keys,
    reference_values,
    reference_live,
):
    far1_keys = fetch(in_hbm(key_rows), far_first)
    near_values = fetch(values, beside)
    rows = pack_rows(reference_live, reference_keys, reference_values)
    far1_values = fetch(values, far_first)
    rows = column_rows(rows)
    own_squares = square_sums("own_squares", (queries, key_rows), rows)
    normed_queries, normed_keys = prepare(queries, key_rows, (query_gain, key_gain), own_squares)
    near_keys = fetch(normed_keys, beside)
    far1_squares = square_sums("far_squares", (far1_keys,), (near_values,))
    far1_packed = prepare_far(far1_keys, key_gain, far1_squares, rows)

    passed_packed = fetch(after(far1_packed, near_values, near_keys), beside)
    far2_keys = fetch(after(normed_keys, far1_values), far_second)
    far2_values = fetch(after(values, far1_values), far_second)
    passed_values = fetch(far1_values, beside)

    state = attend_early(
        pattern,
        normed_queries,
        (normed_keys, near_keys, far1_packed),
        (values, near_values, far1_values),
    )
    inverses, partial, weights = attend_late_keys(
        pattern, normed_queries, far1_packed, passed_packed, far2_keys, state
    )
    return attend_late_values(inverses, partial, weights, (passed_values, far2_values))


def solution(mesh):
    in_specs = (
        P(("grp", "frm"), "tp"),
        P(("grp", "frm"), "tp"),
        P(("grp", "frm"), "tp"),
        P("tp"),
        P("tp"),
        P(("grp", "frm"), None),
        P(("grp", "frm"), "tp"),
        P(("grp", "frm"), "tp"),
        P(("grp", "frm")),
    )
    out_specs = P(("grp", "frm"), "tp")
    return jax.shard_map(shards, mesh=mesh, in_specs=in_specs, out_specs=out_specs, check_vma=False)
```

```python
import math

import jax
import jax.numpy as jnp
from jax import lax
from jax.experimental import pallas as pl
from jax.experimental.pallas import tpu as pltpu
from jax.sharding import PartitionSpec as P

HEADS = 20
HEAD_DIM = 128
WINDOW = 2
EPSILON = 1e-06
LANES = 128
SCRATCH_BYTES = 24 * 2**20
DEAD = float("inf")
TO_LOG2 = HEAD_DIM ** (-0.5) * math.log2(math.e)


def fetch(block, source_of, axis="frm"):
    n = lax.axis_size(axis)
    return lax.ppermute(block, axis, [(source_of(i) % n, i) for i in range(n)])


def after(value, *earlier):
    return lax.optimization_barrier((value,) + earlier)[0]


def far_first(i):
    return i + WINDOW if i % 2 == 0 else i - WINDOW


def far_second(i):
    return i - WINDOW if i % 2 == 0 else i + WINDOW


def beside(i):
    return i + 1 if i % 2 == 0 else i - 1


def in_vmem(array):
    return pltpu.with_memory_space_constraint(array, pltpu.VMEM)


def in_hbm(array):
    return pltpu.with_memory_space_constraint(array, pltpu.HBM)


VMEM = pl.BlockSpec(memory_space=pltpu.VMEM)
SMEM = pl.BlockSpec(memory_space=pltpu.SMEM)
PARAMS = pltpu.CompilerParams(vmem_limit_bytes=SCRATCH_BYTES)


CHEAP = pl.CostEstimate(flops=1, transcendentals=0, bytes_accessed=1)


def head_columns(head):
    return slice(head * HEAD_DIM, (head + 1) * HEAD_DIM)


def score(queries, keys):
    return lax.dot_general(
        queries, keys, (((1,), (1,)), ((), ())), preferred_element_type=jnp.float32
    )


def pack_kernel(live_ref, keys_ref, values_ref, rows_ref, sems):
    slots, features = keys_ref.shape
    copies = [
        pltpu.make_async_copy(keys_ref, rows_ref.at[:, :features], sems.at[0]),
        pltpu.make_async_copy(values_ref, rows_ref.at[:, features:], sems.at[1]),
    ]
    for copy in copies:
        copy.start()
    for copy in copies:
        copy.wait()
    slot = lax.broadcasted_iota(jnp.int32, (slots, features), 0)
    keys = rows_ref[:, :features].astype(jnp.float32)
    rows_ref[:, :features] = jnp.where(slot < live_ref[0], keys, DEAD).astype(jnp.bfloat16)


def pack_rows(live, keys, values):
    slots, features = keys.shape
    return pl.pallas_call(
        pack_kernel,
        out_shape=pltpu.VMEM((slots, 2 * features), jnp.bfloat16),
        in_specs=[SMEM] + [pl.BlockSpec(memory_space=pltpu.HBM)] * 2,
        out_specs=VMEM,
        scratch_shapes=[pltpu.SemaphoreType.DMA((2,))],
        compiler_params=PARAMS,
        cost_estimate=CHEAP,
        name="pack_rows",
    )(live, in_hbm(keys), in_hbm(values))


def squares_kernel(*refs):
    *row_refs, squares_ref = refs
    lane = lax.broadcasted_iota(jnp.int32, squares_ref.shape, 1)
    squares = jnp.zeros(squares_ref.shape, jnp.float32)
    for column, ref in enumerate(row_refs):
        rows = ref[...].astype(jnp.float32)
        squares = jnp.where(lane == column, jnp.sum(rows * rows, axis=1, keepdims=True), squares)
    squares_ref[...] = squares


def square_sums(name, blocks, earlier=()):
    squares = pl.pallas_call(
        squares_kernel,
        out_shape=pltpu.VMEM((blocks[0].shape[0], LANES), jnp.float32),
        in_specs=[VMEM] * len(blocks),
        out_specs=VMEM,
        compiler_params=PARAMS,
        cost_estimate=CHEAP,
        name=name,
    )(*map(in_vmem, blocks))
    squares = after(squares, *earlier)
    return squares, fetch(squares, lambda i: i ^ 1, "tp")


def normalized(rows_ref, gain_ref, squares_refs, column):
    square_sum = sum(ref[:, column : column + 1] for ref in squares_refs)
    scale = lax.rsqrt(square_sum / (HEADS * HEAD_DIM) + EPSILON)
    rows = rows_ref[...].astype(jnp.float32)
    return (rows * scale * gain_ref[...][None, :]).astype(jnp.bfloat16)


def prepare_kernel(
    queries, keys, query_gain, key_gain, squares, other_squares, query_ref, key_ref
):
    query_ref[...] = normalized(queries, query_gain, (squares, other_squares), 0)
    key_ref[...] = normalized(keys, key_gain, (squares, other_squares), 1)


def prepare(queries, keys, gains, squares):
    return pl.pallas_call(
        prepare_kernel,
        out_shape=(pltpu.VMEM(keys.shape, jnp.bfloat16),) * 2,
        in_specs=[VMEM] * 6,
        out_specs=(VMEM,) * 2,
        compiler_params=PARAMS,
        cost_estimate=CHEAP,
        name="prepare",
    )(*map(in_vmem, (queries, keys, *gains, *squares)))


def prepare_far_kernel(keys, gain, squares, other_squares, *refs):
    *row_refs, packed_ref = refs
    tokens, features = keys.shape
    count = (packed_ref.shape[0] - tokens) // 2
    packed_ref[:tokens] = normalized(keys, gain, (squares, other_squares), 0)
    first = tokens
    for ref in row_refs:
        slots = ref.shape[0]
        packed_ref[first : first + slots] = ref[:, :features]
        packed_ref[first + count : first + count + slots] = ref[:, features:]
        first += slots


def prepare_far(keys, gain, squares, rows):
    tokens, features = keys.shape
    count = sum(part.shape[0] for part in rows)
    return pl.pallas_call(
        prepare_far_kernel,
        out_shape=pltpu.VMEM((tokens + 2 * count, features), jnp.bfloat16),
        in_specs=[VMEM] * (4 + len(rows)),
        out_specs=VMEM,
        compiler_params=PARAMS,
        cost_estimate=CHEAP,
        name="prepare_far",
    )(*map(in_vmem, (keys, gain, *squares, *rows)))


def pattern_flag(pattern_ref, column):
    even = lax.rem(lax.axis_index("frm"), 2) == 0
    return jnp.where(even, pattern_ref[0, 2 * WINDOW - 1 - column], pattern_ref[0, column]) > 0


def block_bias(flag, tokens):
    return jnp.where(flag, jnp.zeros((1, tokens), jnp.float32), -jnp.inf)


def softmax_parts(scores_ref, head, bias):
    scores = jnp.where(bias < 0, bias, scores_ref[head] * TO_LOG2)
    return scores, jnp.max(scores, axis=1, keepdims=True)


def early_kernel(
    pattern_ref,
    query_ref,
    own_keys,
    near_keys,
    far_packed,
    own_values,
    near_values,
    far_values,
    peaks_ref,
    totals_ref,
    partial_ref,
    scores_ref,
    weights_ref,
):
    tokens, features = query_ref.shape
    heads = features // HEAD_DIM
    bias = jnp.concatenate(
        [
            jnp.zeros((1, tokens), jnp.float32),
            block_bias(pattern_flag(pattern_ref, 1), tokens),
            block_bias(pattern_flag(pattern_ref, 0), tokens),
        ],
        axis=1,
    )
    for head in range(heads):
        columns = head_columns(head)
        keys = [own_keys[:, columns], near_keys[:, columns], far_packed[:tokens, columns]]
        scores_ref[head] = score(query_ref[:, columns], jnp.concatenate(keys, axis=0))
    for head in range(heads):
        scores, peak = softmax_parts(scores_ref, head, bias)
        weights = jnp.exp2(scores - peak)
        total = jnp.sum(weights, axis=1, keepdims=True)
        weights_ref[head] = weights.astype(jnp.bfloat16)
        peaks_ref[head] = jnp.broadcast_to(peak, (tokens, LANES))
        totals_ref[head] = jnp.broadcast_to(total, (tokens, LANES))
    for head in range(heads):
        columns = head_columns(head)
        values = [ref[:, columns] for ref in (own_values, near_values, far_values)]
        partial_ref[:, columns] = jnp.dot(
            weights_ref[head],
            jnp.concatenate(values, axis=0),
            preferred_element_type=jnp.float32,
        )


def late_keys_kernel(
    pattern_ref,
    query_ref,
    own_packed,
    passed_packed,
    far_keys,
    old_peaks_ref,
    old_totals_ref,
    old_partial_ref,
    inverses_ref,
    partial_ref,
    weights_ref,
    keys_ref,
    values_ref,
    scores_ref,
):
    tokens, features = query_ref.shape
    heads = features // HEAD_DIM
    blocks = 2 * tokens
    count = values_ref.shape[0] // 2
    keys_ref[:tokens] = passed_packed[:tokens]
    keys_ref[tokens:blocks] = far_keys[...]
    for place, packed in enumerate((own_packed, passed_packed)):
        first = place * count
        keys_ref[blocks + first : blocks + first + count] = packed[tokens : tokens + count]
        values_ref[first : first + count] = packed[tokens + count :]
    marks = score(jnp.ones((8, LANES), jnp.bfloat16), keys_ref[blocks:, :LANES])
    bias = jnp.concatenate(
        [
            block_bias(pattern_flag(pattern_ref, 2), tokens),
            block_bias(pattern_flag(pattern_ref, 3), tokens),
            jnp.where(jnp.abs(marks[:1]) < DEAD, 0.0, -jnp.inf),
        ],
        axis=1,
    )
    for head in range(heads):
        columns = head_columns(head)
        scores_ref[head] = score(query_ref[:, columns], keys_ref[:, columns])
    for head in range(heads):
        columns = head_columns(head)
        scores, peak = softmax_parts(scores_ref, head, bias)
        old_peak = old_peaks_ref[head]
        peak = jnp.maximum(old_peak, peak)
        weights = jnp.exp2(scores - peak[:, :1])
        fading = jnp.exp2(old_peak - peak)
        total = jnp.sum(weights, axis=1, keepdims=True)
        inverse = 1.0 / (old_totals_ref[head] * fading + total)
        inverses_ref[head] = inverse
        weights = weights.astype(jnp.bfloat16)
        weights_ref[head] = weights[:, :blocks]
        product = jnp.dot(
            weights[:, blocks:], values_ref[:, columns], preferred_element_type=jnp.float32
        )
        partial_ref[:, columns] = (old_partial_ref[:, columns] * fading + product) * inverse


def late_values_kernel(
    inverses_ref, partial_ref, weights_ref, passed_values, far_values, out_ref, out_vmem, sems
):
    heads = weights_ref.shape[0]
    copies = []
    for head in range(heads):
        columns = head_columns(head)
        values = jnp.concatenate([passed_values[:, columns], far_values[:, columns]], axis=0)
        product = jnp.dot(weights_ref[head], values, preferred_element_type=jnp.float32)
        out_vmem[:, columns] = (
            partial_ref[:, columns] + product * inverses_ref[head]
        ).astype(jnp.bfloat16)
        copy = pltpu.make_async_copy(
            out_vmem.at[:, columns], out_ref.at[:, columns], sems.at[head]
        )
        copy.start()
        copies.append(copy)
    for copy in copies:
        copy.wait()


def attend_early(pattern, queries, keys, values):
    tokens, features = queries.shape
    heads = features // HEAD_DIM
    count = 3 * tokens
    return pl.pallas_call(
        early_kernel,
        out_shape=(
            pltpu.VMEM((heads, tokens, LANES), jnp.float32),
            pltpu.VMEM((heads, tokens, LANES), jnp.float32),
            pltpu.VMEM((tokens, features), jnp.float32),
        ),
        in_specs=[SMEM] + [VMEM] * 7,
        out_specs=(VMEM,) * 3,
        scratch_shapes=[
            pltpu.VMEM((heads, tokens, count), jnp.float32),
            pltpu.VMEM((heads, tokens, count), jnp.bfloat16),
        ],
        compiler_params=PARAMS,
        cost_estimate=CHEAP,
        name="attend_early",
    )(pattern, *map(in_vmem, (queries, *keys, *values)))


def attend_late_keys(pattern, queries, own_packed, passed_packed, far_keys, state):
    tokens, features = queries.shape
    heads = features // HEAD_DIM
    rows = own_packed.shape[0] - tokens
    count = 2 * tokens + rows
    return pl.pallas_call(
        late_keys_kernel,
        out_shape=(
            pltpu.VMEM((heads, tokens, LANES), jnp.float32),
            pltpu.VMEM((tokens, features), jnp.float32),
            pltpu.VMEM((heads, tokens, 2 * tokens), jnp.bfloat16),
        ),
        in_specs=[SMEM] + [VMEM] * 7,
        out_specs=(VMEM,) * 3,
        scratch_shapes=[
            pltpu.VMEM((count, features), jnp.bfloat16),
            pltpu.VMEM((rows, features), jnp.bfloat16),
            pltpu.VMEM((heads, tokens, count), jnp.float32),
        ],
        compiler_params=PARAMS,
        cost_estimate=CHEAP,
        name="attend_late_keys",
    )(pattern, *map(in_vmem, (queries, own_packed, passed_packed, far_keys, *state)))


def attend_late_values(inverses, partial, weights, values):
    tokens, features = partial.shape
    heads = features // HEAD_DIM
    return pl.pallas_call(
        late_values_kernel,
        out_shape=jax.ShapeDtypeStruct((tokens, features), jnp.bfloat16),
        in_specs=[VMEM] * 5,
        out_specs=pl.BlockSpec(memory_space=pl.ANY),
        scratch_shapes=[
            pltpu.VMEM((tokens, features), jnp.bfloat16),
            pltpu.SemaphoreType.DMA((heads,)),
        ],
        compiler_params=PARAMS,
        cost_estimate=CHEAP,
        name="attend_late_values",
    )(*map(in_vmem, (inverses, partial, weights, *values)))


def column_rows(rows):
    n = lax.axis_size("frm")
    if n <= 8:
        return [rows] + [fetch(rows, lambda i: i + distance) for distance in range(2, n, 2)]
    distance = n // 2
    while distance > 1:
        rows = jnp.concatenate([rows, fetch(rows, lambda i: i ^ distance)], axis=0)
        distance //= 2
    return [rows]


def shards(
    queries,
    key_rows,
    values,
    query_gain,
    key_gain,
    pattern,
    reference_keys,
    reference_values,
    reference_live,
):
    far1_keys = fetch(in_hbm(key_rows), far_first)
    near_values = fetch(values, beside)
    rows = pack_rows(reference_live, reference_keys, reference_values)
    far1_values = fetch(values, far_first)
    rows = column_rows(rows)
    own_squares = square_sums("own_squares", (queries, key_rows), rows)
    normed_queries, normed_keys = prepare(queries, key_rows, (query_gain, key_gain), own_squares)
    near_keys = fetch(normed_keys, beside)
    far1_squares = square_sums("far_squares", (far1_keys,), (near_values,))
    far1_packed = prepare_far(far1_keys, key_gain, far1_squares, rows)

    passed_packed = fetch(after(far1_packed, near_values, near_keys), beside)
    far2_keys = fetch(after(normed_keys, near_keys), far_second)
    far2_values = fetch(after(values, far1_values), far_second)
    passed_values = fetch(far1_values, beside)

    state = attend_early(
        pattern,
        normed_queries,
        (normed_keys, near_keys, far1_packed),
        (values, near_values, far1_values),
    )
    inverses, partial, weights = attend_late_keys(
        pattern, normed_queries, far1_packed, passed_packed, far2_keys, state
    )
    return attend_late_values(inverses, partial, weights, (passed_values, far2_values))


def solution(mesh):
    in_specs = (
        P(("grp", "frm"), "tp"),
        P(("grp", "frm"), "tp"),
        P(("grp", "frm"), "tp"),
        P("tp"),
        P("tp"),
        P(("grp", "frm"), None),
        P(("grp", "frm"), "tp"),
        P(("grp", "frm"), "tp"),
        P(("grp", "frm")),
    )
    out_specs = P(("grp", "frm"), "tp")
    return jax.shard_map(shards, mesh=mesh, in_specs=in_specs, out_specs=out_specs, check_vma=False)
```

```python
import math

import jax
import jax.numpy as jnp
from jax import lax
from jax.experimental import pallas as pl
from jax.experimental.pallas import tpu as pltpu
from jax.sharding import PartitionSpec as P

HEADS = 20
HEAD_DIM = 128
WINDOW = 2
EPSILON = 1e-06
LANES = 128
SCRATCH_BYTES = 24 * 2**20
DEAD = float("inf")
TO_LOG2 = HEAD_DIM ** (-0.5) * math.log2(math.e)


def fetch(block, source_of, axis="frm"):
    n = lax.axis_size(axis)
    return lax.ppermute(block, axis, [(source_of(i) % n, i) for i in range(n)])


def after(value, *earlier):
    return lax.optimization_barrier((value,) + earlier)[0]


def far_first(i):
    return i + WINDOW if i % 2 == 0 else i - WINDOW


def far_second(i):
    return i - WINDOW if i % 2 == 0 else i + WINDOW


def beside(i):
    return i + 1 if i % 2 == 0 else i - 1


def in_vmem(array):
    return pltpu.with_memory_space_constraint(array, pltpu.VMEM)


def in_hbm(array):
    return pltpu.with_memory_space_constraint(array, pltpu.HBM)


VMEM = pl.BlockSpec(memory_space=pltpu.VMEM)
SMEM = pl.BlockSpec(memory_space=pltpu.SMEM)
PARAMS = pltpu.CompilerParams(vmem_limit_bytes=SCRATCH_BYTES)


CHEAP = pl.CostEstimate(flops=1, transcendentals=0, bytes_accessed=1)

EARLY = pl.CostEstimate(flops=5*10**9, transcendentals=0, bytes_accessed=1)
SMALL_HOLD = pl.CostEstimate(flops=2*10**9, transcendentals=0, bytes_accessed=1)
HOLD = pl.CostEstimate(flops=3 * 10**10, transcendentals=0, bytes_accessed=1)


def head_columns(head):
    return slice(head * HEAD_DIM, (head + 1) * HEAD_DIM)


def score(queries, keys):
    return lax.dot_general(
        queries, keys, (((1,), (1,)), ((), ())), preferred_element_type=jnp.float32
    )


def pack_kernel(live_ref, keys_ref, values_ref, rows_ref, sems):
    slots, features = keys_ref.shape
    copies = [
        pltpu.make_async_copy(keys_ref, rows_ref.at[:, :features], sems.at[0]),
        pltpu.make_async_copy(values_ref, rows_ref.at[:, features:], sems.at[1]),
    ]
    for copy in copies:
        copy.start()
    for copy in copies:
        copy.wait()
    slot = lax.broadcasted_iota(jnp.int32, (slots, features), 0)
    keys = rows_ref[:, :features].astype(jnp.float32)
    rows_ref[:, :features] = jnp.where(slot < live_ref[0], keys, DEAD).astype(jnp.bfloat16)


def pack_rows(live, keys, values):
    slots, features = keys.shape
    return pl.pallas_call(
        pack_kernel,
        out_shape=pltpu.VMEM((slots, 2 * features), jnp.bfloat16),
        in_specs=[SMEM] + [pl.BlockSpec(memory_space=pltpu.HBM)] * 2,
        out_specs=VMEM,
        scratch_shapes=[pltpu.SemaphoreType.DMA((2,))],
        compiler_params=PARAMS,
        cost_estimate=CHEAP,
        name="pack_rows",
    )(live, in_hbm(keys), in_hbm(values))


def load_kernel(*refs):
    sources, loaded = refs[:4], refs[4:8]
    squares_ref, sems = refs[8:]
    copies = [
        pltpu.make_async_copy(source, target, sems.at[i])
        for i, (source, target) in enumerate(zip(sources, loaded))
    ]
    for copy in copies:
        copy.start()
    lane = lax.broadcasted_iota(jnp.int32, squares_ref.shape, 1)
    squares = jnp.zeros(squares_ref.shape, jnp.float32)
    for column, copy in enumerate(copies):
        copy.wait()
        if column < 2:
            rows = loaded[column][...].astype(jnp.float32)
            sums = jnp.sum(rows * rows, axis=1, keepdims=True)
            squares = jnp.where(lane == column, sums, squares)
    squares_ref[...] = squares


def load(queries, keys, gains):
    operands = (queries, keys, *gains)
    return pl.pallas_call(
        load_kernel,
        out_shape=(
            *(pltpu.VMEM(operand.shape, operand.dtype) for operand in operands),
            pltpu.VMEM((queries.shape[0], LANES), jnp.float32),
        ),
        in_specs=[pl.BlockSpec(memory_space=pltpu.HBM)] * 4,
        out_specs=(VMEM,) * 5,
        scratch_shapes=[pltpu.SemaphoreType.DMA((4,))],
        compiler_params=PARAMS,
        cost_estimate=CHEAP,
        name="load",
    )(*map(in_hbm, operands))


def normalized(rows_ref, gain_ref, squares_refs, column):
    square_sum = sum(ref[:, column : column + 1] for ref in squares_refs)
    scale = lax.rsqrt(square_sum / (HEADS * HEAD_DIM) + EPSILON)
    rows = rows_ref[: scale.shape[0]].astype(jnp.float32)
    return (rows * scale * gain_ref[...][None, :]).astype(jnp.bfloat16)


def prepare_kernel(queries, keys, query_gain, key_gain, squares, other_squares, *refs):
    *row_refs, query_ref, key_ref, packed_ref, pair_ref = refs
    tokens, features = keys.shape
    query_ref[...] = normalized(queries, query_gain, (squares, other_squares), 0)
    normed_keys = normalized(keys, key_gain, (squares, other_squares), 1)
    key_ref[...] = normed_keys
    packed_ref[:tokens] = normed_keys
    count = pair_ref.shape[0]
    first = 0
    for ref in row_refs:
        pair_ref[first : first + ref.shape[0]] = ref[...]
        first += ref.shape[0]
    packed_ref[tokens : tokens + count] = pair_ref[:, :features]
    packed_ref[tokens + count :] = pair_ref[:, features:]


def prepare(queries, keys, gains, squares, rows):
    tokens, features = keys.shape
    count = sum(part.shape[0] for part in rows)
    return pl.pallas_call(
        prepare_kernel,
        out_shape=(
            pltpu.VMEM((tokens, features), jnp.bfloat16),
            pltpu.VMEM((tokens, features), jnp.bfloat16),
            pltpu.VMEM((tokens + 2 * count, features), jnp.bfloat16),
            pltpu.VMEM((count, 2 * features), jnp.bfloat16),
        ),
        in_specs=[VMEM] * (6 + len(rows)),
        out_specs=(VMEM,) * 4,
        compiler_params=PARAMS,
        cost_estimate=CHEAP,
        name="prepare",
    )(*map(in_vmem, (queries, keys, *gains, *squares, *rows)))


def halve_kernel(rows, first_ref, second_ref):
    half = first_ref.shape[0]
    first_ref[...] = rows[:half]
    second_ref[...] = rows[half:]


def halve(rows):
    half = pltpu.VMEM((rows.shape[0] // 2, rows.shape[1]), rows.dtype)
    return pl.pallas_call(
        halve_kernel,
        out_shape=(half, half),
        in_specs=[VMEM],
        out_specs=(VMEM,) * 2,
        compiler_params=PARAMS,
        cost_estimate=CHEAP,
        name="halve",
    )(in_vmem(rows))


def strip_kernel(packed, key_ref):
    key_ref[...] = packed[: key_ref.shape[0]]


def strip(packed, tokens, cost=None):
    return pl.pallas_call(
        strip_kernel,
        out_shape=pltpu.VMEM((tokens, packed.shape[1]), jnp.bfloat16),
        in_specs=[VMEM],
        out_specs=VMEM,
        compiler_params=PARAMS,
        cost_estimate=cost or CHEAP,
        name="strip",
    )(in_vmem(packed))


def pattern_flag(pattern_ref, column):
    even = lax.rem(lax.axis_index("frm"), 2) == 0
    return jnp.where(even, pattern_ref[0, 2 * WINDOW - 1 - column], pattern_ref[0, column]) > 0


def block_bias(flag, tokens):
    return jnp.where(flag, jnp.zeros((1, tokens), jnp.float32), -jnp.inf)


def softmax_parts(scores_ref, head, bias):
    scores = jnp.where(bias < 0, bias, scores_ref[head] * TO_LOG2)
    return scores, jnp.max(scores, axis=1, keepdims=True)


def early_kernel(
    pattern_ref,
    query_ref,
    own_keys,
    near_keys,
    far_keys,
    own_values,
    near_values,
    far_values,
    peaks_ref,
    totals_ref,
    partial_ref,
    scores_ref,
    weights_ref,
):
    tokens, features = query_ref.shape
    heads = features // HEAD_DIM
    bias = jnp.concatenate(
        [
            jnp.zeros((1, tokens), jnp.float32),
            block_bias(pattern_flag(pattern_ref, 1), tokens),
            block_bias(pattern_flag(pattern_ref, 0), tokens),
        ],
        axis=1,
    )
    for head in range(heads):
        columns = head_columns(head)
        keys = [ref[:, columns] for ref in (own_keys, near_keys, far_keys)]
        scores_ref[head] = score(query_ref[:, columns], jnp.concatenate(keys, axis=0))
    for head in range(heads):
        scores, peak = softmax_parts(scores_ref, head, bias)
        weights = jnp.exp2(scores - peak)
        total = jnp.sum(weights, axis=1, keepdims=True)
        weights_ref[head] = weights.astype(jnp.bfloat16)
        peaks_ref[head] = jnp.broadcast_to(peak, (tokens, LANES))
        totals_ref[head] = jnp.broadcast_to(total, (tokens, LANES))
    for head in range(heads):
        columns = head_columns(head)
        values = [ref[:, columns] for ref in (own_values, near_values, far_values)]
        partial_ref[:, columns] = jnp.dot(
            weights_ref[head],
            jnp.concatenate(values, axis=0),
            preferred_element_type=jnp.float32,
        )


def late_keys_kernel(
    pattern_ref,
    query_ref,
    passed_keys,
    far_packed,
    far1_packed,
    old_peaks_ref,
    old_totals_ref,
    old_partial_ref,
    *refs,
):
    *row_refs, inverses_ref, partial_ref, weights_ref, keys_ref, values_ref, scores_ref = refs
    tokens, features = query_ref.shape
    heads = features // HEAD_DIM
    blocks = 2 * tokens
    keys_ref[:tokens] = passed_keys[...]
    keys_ref[tokens:blocks] = far_packed[:tokens]
    first = 0
    for ref in row_refs:
        count = ref.shape[0]
        keys_ref[blocks + first : blocks + first + count] = ref[:, :features]
        values_ref[first : first + count] = ref[:, features:]
        first += count
    for packed in (far_packed, far1_packed):
        count = (packed.shape[0] - tokens) // 2
        if count:
            keys_ref[blocks + first : blocks + first + count] = packed[tokens : tokens + count]
            values_ref[first : first + count] = packed[tokens + count :]
            first += count
    marks = score(jnp.ones((8, LANES), jnp.bfloat16), keys_ref[blocks:, :LANES])
    bias = jnp.concatenate(
        [
            block_bias(pattern_flag(pattern_ref, 2), tokens),
            block_bias(pattern_flag(pattern_ref, 3), tokens),
            jnp.where(jnp.abs(marks[:1]) < DEAD, 0.0, -jnp.inf),
        ],
        axis=1,
    )
    for head in range(heads):
        columns = head_columns(head)
        scores_ref[head] = score(query_ref[:, columns], keys_ref[:, columns])
    for head in range(heads):
        columns = head_columns(head)
        scores, peak = softmax_parts(scores_ref, head, bias)
        old_peak = old_peaks_ref[head]
        peak = jnp.maximum(old_peak, peak)
        weights = jnp.exp2(scores - peak[:, :1])
        fading = jnp.exp2(old_peak - peak)
        total = jnp.sum(weights, axis=1, keepdims=True)
        inverse = 1.0 / (old_totals_ref[head] * fading + total)
        inverses_ref[head] = inverse
        weights = weights.astype(jnp.bfloat16)
        weights_ref[head] = weights[:, :blocks]
        product = jnp.dot(
            weights[:, blocks:], values_ref[:, columns], preferred_element_type=jnp.float32
        )
        partial_ref[:, columns] = (old_partial_ref[:, columns] * fading + product) * inverse


def late_values_kernel(
    inverses_ref, partial_ref, weights_ref, first_half, second_half, far_values, out_ref, out_vmem, sems
):
    heads = weights_ref.shape[0]
    copies = []
    for head in range(heads):
        columns = head_columns(head)
        values = jnp.concatenate(
            [ref[:, columns] for ref in (first_half, second_half, far_values)], axis=0
        )
        product = jnp.dot(weights_ref[head], values, preferred_element_type=jnp.float32)
        out_vmem[:, columns] = (
            partial_ref[:, columns] + product * inverses_ref[head]
        ).astype(jnp.bfloat16)
        copy = pltpu.make_async_copy(
            out_vmem.at[:, columns], out_ref.at[:, columns], sems.at[head]
        )
        copy.start()
        copies.append(copy)
    for copy in copies:
        copy.wait()


def attend_early(pattern, queries, keys, values):
    tokens, features = queries.shape
    heads = features // HEAD_DIM
    count = 3 * tokens
    return pl.pallas_call(
        early_kernel,
        out_shape=(
            pltpu.VMEM((heads, tokens, LANES), jnp.float32),
            pltpu.VMEM((heads, tokens, LANES), jnp.float32),
            pltpu.VMEM((tokens, features), jnp.float32),
        ),
        in_specs=[SMEM] + [VMEM] * 7,
        out_specs=(VMEM,) * 3,
        scratch_shapes=[
            pltpu.VMEM((heads, tokens, count), jnp.float32),
            pltpu.VMEM((heads, tokens, count), jnp.bfloat16),
        ],
        compiler_params=PARAMS,
        cost_estimate=EARLY,
        name="attend_early",
    )(pattern, *map(in_vmem, (queries, *keys, *values)))


def attend_late_keys(pattern, queries, passed_keys, far_packed, far1_packed, rows, state):
    tokens, features = queries.shape
    heads = features // HEAD_DIM
    attached = (far_packed.shape[0] + far1_packed.shape[0]) // 2 - tokens
    slots = attached + sum(part.shape[0] for part in rows)
    count = 2 * tokens + slots
    operands = (queries, passed_keys, far_packed, far1_packed, *state, *rows)
    return pl.pallas_call(
        late_keys_kernel,
        out_shape=(
            pltpu.VMEM((heads, tokens, LANES), jnp.float32),
            pltpu.VMEM((tokens, features), jnp.float32),
            pltpu.VMEM((heads, tokens, 2 * tokens), jnp.bfloat16),
        ),
        in_specs=[SMEM] + [VMEM] * len(operands),
        out_specs=(VMEM,) * 3,
        scratch_shapes=[
            pltpu.VMEM((count, features), jnp.bfloat16),
            pltpu.VMEM((slots, features), jnp.bfloat16),
            pltpu.VMEM((heads, tokens, count), jnp.float32),
        ],
        compiler_params=PARAMS,
        cost_estimate=CHEAP,
        name="attend_late_keys",
    )(pattern, *map(in_vmem, operands))


def attend_late_values(inverses, partial, weights, values):
    tokens, features = partial.shape
    heads = features // HEAD_DIM
    return pl.pallas_call(
        late_values_kernel,
        out_shape=jax.ShapeDtypeStruct((tokens, features), jnp.bfloat16),
        in_specs=[VMEM] * 6,
        out_specs=pl.BlockSpec(memory_space=pl.ANY),
        scratch_shapes=[
            pltpu.VMEM((tokens, features), jnp.bfloat16),
            pltpu.SemaphoreType.DMA((heads,)),
        ],
        compiler_params=PARAMS,
        cost_estimate=CHEAP,
        name="attend_late_values",
    )(*map(in_vmem, (inverses, partial, weights, *values)))


def other_rows(pair):
    n = lax.axis_size("frm")
    return [fetch(pair, lambda i: i + distance) for distance in range(4, n - 2, 2)]


def shards(
    queries,
    key_rows,
    values,
    query_gain,
    key_gain,
    pattern,
    reference_keys,
    reference_values,
    reference_live,
):
    tokens = queries.shape[0]
    far1_values = fetch(values, far_first)
    rows = pack_rows(reference_live, reference_keys, reference_values)
    rows = [rows, fetch(rows, beside)]
    near_values = fetch(after(values, *rows), beside)
    *loaded, squares = load(queries, key_rows, (query_gain, key_gain))
    own_squares = (squares, fetch(squares, lambda i: i ^ 1, "tp"))
    normed_queries, normed_keys, packed_keys, pair = prepare(
        *loaded[:2], loaded[2:], own_squares, rows
    )
    near_keys = fetch(normed_keys, beside)
    far1_packed = fetch(packed_keys, far_first)
    held = strip(after(pair, far1_values), pair.shape[0], SMALL_HOLD)
    held = strip(after(held, near_values), pair.shape[0], HOLD)
    rows = [pair] + other_rows(held)

    far1_keys = strip(far1_packed, tokens)
    passed_keys = fetch(after(far1_keys, near_keys, *rows), beside)
    far2_packed = fetch(after(packed_keys, far1_packed), far_second)
    far2_values = fetch(after(values, far1_keys), far_second)
    first_half, second_half = halve(far1_values)
    passed_first = fetch(first_half, beside)
    passed_second = fetch(after(second_half, far1_keys), beside)

    state = attend_early(
        pattern,
        after(normed_queries, passed_first),
        (normed_keys, near_keys, far1_keys),
        (values, near_values, far1_values),
    )
    inverses, partial, weights = attend_late_keys(
        pattern, normed_queries, passed_keys, far2_packed, far1_packed, rows, state
    )
    return attend_late_values(inverses, partial, weights, (passed_first, passed_second, far2_values))


def solution(mesh):
    in_specs = (
        P(("grp", "frm"), "tp"),
        P(("grp", "frm"), "tp"),
        P(("grp", "frm"), "tp"),
        P("tp"),
        P("tp"),
        P(("grp", "frm"), None),
        P(("grp", "frm"), "tp"),
        P(("grp", "frm"), "tp"),
        P(("grp", "frm")),
    )
    out_specs = P(("grp", "frm"), "tp")
    return jax.shard_map(shards, mesh=mesh, in_specs=in_specs, out_specs=out_specs, check_vma=False)
```

```python
import math

import jax
import jax.numpy as jnp
from jax import lax
from jax.experimental import pallas as pl
from jax.experimental.pallas import tpu as pltpu
from jax.sharding import PartitionSpec as P

HEADS = 20
HEAD_DIM = 128
WINDOW = 2
EPSILON = 1e-06
LANES = 128
SCRATCH_BYTES = 24 * 2**20
DEAD = float("inf")
TO_LOG2 = HEAD_DIM ** (-0.5) * math.log2(math.e)


def fetch(block, source_of, axis="frm"):
    n = lax.axis_size(axis)
    return lax.ppermute(block, axis, [(source_of(i) % n, i) for i in range(n)])


def after(value, *earlier):
    return lax.optimization_barrier((value,) + earlier)[0]


def far_first(i):
    return i + WINDOW if i % 2 == 0 else i - WINDOW


def far_second(i):
    return i - WINDOW if i % 2 == 0 else i + WINDOW


def beside(i):
    return i + 1 if i % 2 == 0 else i - 1


def in_vmem(array):
    return pltpu.with_memory_space_constraint(array, pltpu.VMEM)


def in_hbm(array):
    return pltpu.with_memory_space_constraint(array, pltpu.HBM)


VMEM = pl.BlockSpec(memory_space=pltpu.VMEM)
SMEM = pl.BlockSpec(memory_space=pltpu.SMEM)
PARAMS = pltpu.CompilerParams(vmem_limit_bytes=SCRATCH_BYTES)


CHEAP = pl.CostEstimate(flops=1, transcendentals=0, bytes_accessed=1)

EARLY = pl.CostEstimate(flops=5*10**9, transcendentals=0, bytes_accessed=1)
HOLD = pl.CostEstimate(flops=8 * 10**9, transcendentals=0, bytes_accessed=1)


def head_columns(head):
    return slice(head * HEAD_DIM, (head + 1) * HEAD_DIM)


def score(queries, keys):
    return lax.dot_general(
        queries, keys, (((1,), (1,)), ((), ())), preferred_element_type=jnp.float32
    )


def pack_kernel(live_ref, keys_ref, values_ref, rows_ref, sems):
    slots, features = keys_ref.shape
    copies = [
        pltpu.make_async_copy(keys_ref, rows_ref.at[:, :features], sems.at[0]),
        pltpu.make_async_copy(values_ref, rows_ref.at[:, features:], sems.at[1]),
    ]
    for copy in copies:
        copy.start()
    for copy in copies:
        copy.wait()
    slot = lax.broadcasted_iota(jnp.int32, (slots, features), 0)
    keys = rows_ref[:, :features].astype(jnp.float32)
    rows_ref[:, :features] = jnp.where(slot < live_ref[0], keys, DEAD).astype(jnp.bfloat16)


def pack_rows(live, keys, values):
    slots, features = keys.shape
    return pl.pallas_call(
        pack_kernel,
        out_shape=pltpu.VMEM((slots, 2 * features), jnp.bfloat16),
        in_specs=[SMEM] + [pl.BlockSpec(memory_space=pltpu.HBM)] * 2,
        out_specs=VMEM,
        scratch_shapes=[pltpu.SemaphoreType.DMA((2,))],
        compiler_params=PARAMS,
        cost_estimate=CHEAP,
        name="pack_rows",
    )(live, in_hbm(keys), in_hbm(values))


def load_kernel(*refs):
    sources, loaded = refs[:4], refs[4:8]
    squares_ref, sems = refs[8:]
    copies = [
        pltpu.make_async_copy(source, target, sems.at[i])
        for i, (source, target) in enumerate(zip(sources, loaded))
    ]
    for copy in copies:
        copy.start()
    lane = lax.broadcasted_iota(jnp.int32, squares_ref.shape, 1)
    squares = jnp.zeros(squares_ref.shape, jnp.float32)
    for column, copy in enumerate(copies):
        copy.wait()
        if column < 2:
            rows = loaded[column][...].astype(jnp.float32)
            sums = jnp.sum(rows * rows, axis=1, keepdims=True)
            squares = jnp.where(lane == column, sums, squares)
    squares_ref[...] = squares


def load(queries, keys, gains):
    operands = (queries, keys, *gains)
    return pl.pallas_call(
        load_kernel,
        out_shape=(
            *(pltpu.VMEM(operand.shape, operand.dtype) for operand in operands),
            pltpu.VMEM((queries.shape[0], LANES), jnp.float32),
        ),
        in_specs=[pl.BlockSpec(memory_space=pltpu.HBM)] * 4,
        out_specs=(VMEM,) * 5,
        scratch_shapes=[pltpu.SemaphoreType.DMA((4,))],
        compiler_params=PARAMS,
        cost_estimate=CHEAP,
        name="load",
    )(*map(in_hbm, operands))


def normalized(rows_ref, gain_ref, squares_refs, column):
    square_sum = sum(ref[:, column : column + 1] for ref in squares_refs)
    scale = lax.rsqrt(square_sum / (HEADS * HEAD_DIM) + EPSILON)
    rows = rows_ref[: scale.shape[0]].astype(jnp.float32)
    return (rows * scale * gain_ref[...][None, :]).astype(jnp.bfloat16)


def prepare_kernel(
    queries, keys, query_gain, key_gain, squares, other_squares, query_ref, key_ref
):
    query_ref[...] = normalized(queries, query_gain, (squares, other_squares), 0)
    key_ref[...] = normalized(keys, key_gain, (squares, other_squares), 1)


def prepare(queries, keys, gains, squares):
    return pl.pallas_call(
        prepare_kernel,
        out_shape=(pltpu.VMEM(keys.shape, jnp.bfloat16),) * 2,
        in_specs=[VMEM] * 6,
        out_specs=(VMEM,) * 2,
        compiler_params=PARAMS,
        cost_estimate=CHEAP,
        name="prepare",
    )(*map(in_vmem, (queries, keys, *gains, *squares)))


def attach_kernel(keys_ref, own_rows, other_rows, packed_ref, pair_ref):
    slots = own_rows.shape[0]
    pair_ref[:slots] = own_rows[...]
    pair_ref[slots:] = other_rows[...]
    tokens, features = keys_ref.shape
    packed_ref[:tokens] = keys_ref[...]
    packed_ref[tokens : tokens + 2 * slots] = pair_ref[:, :features]
    packed_ref[tokens + 2 * slots :] = pair_ref[:, features:]


def attach_rows(keys, own_rows, other_rows):
    tokens, features = keys.shape
    count = 2 * own_rows.shape[0]
    return pl.pallas_call(
        attach_kernel,
        out_shape=(
            pltpu.VMEM((tokens + 2 * count, features), jnp.bfloat16),
            pltpu.VMEM((count, 2 * features), jnp.bfloat16),
        ),
        in_specs=[VMEM] * 3,
        out_specs=(VMEM,) * 2,
        compiler_params=PARAMS,
        cost_estimate=CHEAP,
        name="attach_rows",
    )(*map(in_vmem, (keys, own_rows, other_rows)))


def halve_kernel(rows, first_ref, second_ref):
    half = first_ref.shape[0]
    first_ref[...] = rows[:half]
    second_ref[...] = rows[half:]


def halve(rows):
    half = pltpu.VMEM((rows.shape[0] // 2, rows.shape[1]), rows.dtype)
    return pl.pallas_call(
        halve_kernel,
        out_shape=(half, half),
        in_specs=[VMEM],
        out_specs=(VMEM,) * 2,
        compiler_params=PARAMS,
        cost_estimate=CHEAP,
        name="halve",
    )(in_vmem(rows))


def strip_kernel(packed, key_ref):
    key_ref[...] = packed[: key_ref.shape[0]]


def strip(packed, tokens, cost=None):
    return pl.pallas_call(
        strip_kernel,
        out_shape=pltpu.VMEM((tokens, packed.shape[1]), jnp.bfloat16),
        in_specs=[VMEM],
        out_specs=VMEM,
        compiler_params=PARAMS,
        cost_estimate=cost or CHEAP,
        name="strip",
    )(in_vmem(packed))


def pattern_flag(pattern_ref, column):
    even = lax.rem(lax.axis_index("frm"), 2) == 0
    return jnp.where(even, pattern_ref[0, 2 * WINDOW - 1 - column], pattern_ref[0, column]) > 0


def block_bias(flag, tokens):
    return jnp.where(flag, jnp.zeros((1, tokens), jnp.float32), -jnp.inf)


def softmax_parts(scores_ref, head, bias):
    scores = jnp.where(bias < 0, bias, scores_ref[head] * TO_LOG2)
    return scores, jnp.max(scores, axis=1, keepdims=True)


def early_kernel(
    pattern_ref,
    query_ref,
    own_keys,
    near_keys,
    far_keys,
    own_values,
    near_values,
    far_values,
    peaks_ref,
    totals_ref,
    partial_ref,
    scores_ref,
    weights_ref,
):
    tokens, features = query_ref.shape
    heads = features // HEAD_DIM
    bias = jnp.concatenate(
        [
            jnp.zeros((1, tokens), jnp.float32),
            block_bias(pattern_flag(pattern_ref, 1), tokens),
            block_bias(pattern_flag(pattern_ref, 0), tokens),
        ],
        axis=1,
    )
    for head in range(heads):
        columns = head_columns(head)
        keys = [ref[:, columns] for ref in (own_keys, near_keys, far_keys)]
        scores_ref[head] = score(query_ref[:, columns], jnp.concatenate(keys, axis=0))
    for head in range(heads):
        scores, peak = softmax_parts(scores_ref, head, bias)
        weights = jnp.exp2(scores - peak)
        total = jnp.sum(weights, axis=1, keepdims=True)
        weights_ref[head] = weights.astype(jnp.bfloat16)
        peaks_ref[head] = jnp.broadcast_to(peak, (tokens, LANES))
        totals_ref[head] = jnp.broadcast_to(total, (tokens, LANES))
    for head in range(heads):
        columns = head_columns(head)
        values = [ref[:, columns] for ref in (own_values, near_values, far_values)]
        partial_ref[:, columns] = jnp.dot(
            weights_ref[head],
            jnp.concatenate(values, axis=0),
            preferred_element_type=jnp.float32,
        )


def late_keys_kernel(
    pattern_ref,
    query_ref,
    passed_keys,
    far_packed,
    old_peaks_ref,
    old_totals_ref,
    old_partial_ref,
    *refs,
):
    *row_refs, inverses_ref, partial_ref, weights_ref, keys_ref, values_ref, scores_ref = refs
    tokens, features = query_ref.shape
    heads = features // HEAD_DIM
    blocks = 2 * tokens
    keys_ref[:tokens] = passed_keys[...]
    keys_ref[tokens:blocks] = far_packed[:tokens]
    first = 0
    for ref in row_refs:
        count = ref.shape[0]
        keys_ref[blocks + first : blocks + first + count] = ref[:, :features]
        values_ref[first : first + count] = ref[:, features:]
        first += count
    count = (far_packed.shape[0] - tokens) // 2
    keys_ref[blocks + first :] = far_packed[tokens : tokens + count]
    values_ref[first:] = far_packed[tokens + count :]
    marks = score(jnp.ones((8, LANES), jnp.bfloat16), keys_ref[blocks:, :LANES])
    bias = jnp.concatenate(
        [
            block_bias(pattern_flag(pattern_ref, 2), tokens),
            block_bias(pattern_flag(pattern_ref, 3), tokens),
            jnp.where(jnp.abs(marks[:1]) < DEAD, 0.0, -jnp.inf),
        ],
        axis=1,
    )
    for head in range(heads):
        columns = head_columns(head)
        scores_ref[head] = score(query_ref[:, columns], keys_ref[:, columns])
    for head in range(heads):
        columns = head_columns(head)
        scores, peak = softmax_parts(scores_ref, head, bias)
        old_peak = old_peaks_ref[head]
        peak = jnp.maximum(old_peak, peak)
        weights = jnp.exp2(scores - peak[:, :1])
        fading = jnp.exp2(old_peak - peak)
        total = jnp.sum(weights, axis=1, keepdims=True)
        inverse = 1.0 / (old_totals_ref[head] * fading + total)
        inverses_ref[head] = inverse
        weights = weights.astype(jnp.bfloat16)
        weights_ref[head] = weights[:, :blocks]
        product = jnp.dot(
            weights[:, blocks:], values_ref[:, columns], preferred_element_type=jnp.float32
        )
        partial_ref[:, columns] = (old_partial_ref[:, columns] * fading + product) * inverse


def late_values_kernel(
    inverses_ref, partial_ref, weights_ref, first_half, second_half, far_values, out_ref, out_vmem, sems
):
    heads = weights_ref.shape[0]
    copies = []
    for head in range(heads):
        columns = head_columns(head)
        values = jnp.concatenate(
            [ref[:, columns] for ref in (first_half, second_half, far_values)], axis=0
        )
        product = jnp.dot(weights_ref[head], values, preferred_element_type=jnp.float32)
        out_vmem[:, columns] = (
            partial_ref[:, columns] + product * inverses_ref[head]
        ).astype(jnp.bfloat16)
        copy = pltpu.make_async_copy(
            out_vmem.at[:, columns], out_ref.at[:, columns], sems.at[head]
        )
        copy.start()
        copies.append(copy)
    for copy in copies:
        copy.wait()


def attend_early(pattern, queries, keys, values):
    tokens, features = queries.shape
    heads = features // HEAD_DIM
    count = 3 * tokens
    return pl.pallas_call(
        early_kernel,
        out_shape=(
            pltpu.VMEM((heads, tokens, LANES), jnp.float32),
            pltpu.VMEM((heads, tokens, LANES), jnp.float32),
            pltpu.VMEM((tokens, features), jnp.float32),
        ),
        in_specs=[SMEM] + [VMEM] * 7,
        out_specs=(VMEM,) * 3,
        scratch_shapes=[
            pltpu.VMEM((heads, tokens, count), jnp.float32),
            pltpu.VMEM((heads, tokens, count), jnp.bfloat16),
        ],
        compiler_params=PARAMS,
        cost_estimate=EARLY,
        name="attend_early",
    )(pattern, *map(in_vmem, (queries, *keys, *values)))


def attend_late_keys(pattern, queries, passed_keys, far_packed, rows, state):
    tokens, features = queries.shape
    heads = features // HEAD_DIM
    attached = (far_packed.shape[0] - tokens) // 2
    slots = attached + sum(part.shape[0] for part in rows)
    count = 2 * tokens + slots
    operands = (queries, passed_keys, far_packed, *state, *rows)
    return pl.pallas_call(
        late_keys_kernel,
        out_shape=(
            pltpu.VMEM((heads, tokens, LANES), jnp.float32),
            pltpu.VMEM((tokens, features), jnp.float32),
            pltpu.VMEM((heads, tokens, 2 * tokens), jnp.bfloat16),
        ),
        in_specs=[SMEM] + [VMEM] * len(operands),
        out_specs=(VMEM,) * 3,
        scratch_shapes=[
            pltpu.VMEM((count, features), jnp.bfloat16),
            pltpu.VMEM((slots, features), jnp.bfloat16),
            pltpu.VMEM((heads, tokens, count), jnp.float32),
        ],
        compiler_params=PARAMS,
        cost_estimate=CHEAP,
        name="attend_late_keys",
    )(pattern, *map(in_vmem, operands))


def attend_late_values(inverses, partial, weights, values):
    tokens, features = partial.shape
    heads = features // HEAD_DIM
    return pl.pallas_call(
        late_values_kernel,
        out_shape=jax.ShapeDtypeStruct((tokens, features), jnp.bfloat16),
        in_specs=[VMEM] * 6,
        out_specs=pl.BlockSpec(memory_space=pl.ANY),
        scratch_shapes=[
            pltpu.VMEM((tokens, features), jnp.bfloat16),
            pltpu.SemaphoreType.DMA((heads,)),
        ],
        compiler_params=PARAMS,
        cost_estimate=CHEAP,
        name="attend_late_values",
    )(*map(in_vmem, (inverses, partial, weights, *values)))


def other_rows(pair):
    n = lax.axis_size("frm")
    return [fetch(pair, lambda i: i + distance) for distance in range(4, n - 2, 2)]


def shards(
    queries,
    key_rows,
    values,
    query_gain,
    key_gain,
    pattern,
    reference_keys,
    reference_values,
    reference_live,
):
    tokens = queries.shape[0]
    far1_values = fetch(values, far_first)
    near_values = fetch(values, beside)
    *loaded, squares = load(queries, key_rows, (query_gain, key_gain))
    own_squares = (squares, fetch(squares, lambda i: i ^ 1, "tp"))
    normed_queries, normed_keys = prepare(*loaded[:2], loaded[2:], own_squares)
    near_keys = fetch(normed_keys, beside)
    far1_keys = fetch(normed_keys, far_first)
    own_rows = pack_rows(reference_live, reference_keys, reference_values)
    packed_keys, pair = attach_rows(normed_keys, own_rows, fetch(own_rows, beside))
    held = strip(after(pair, far1_values, near_values), pair.shape[0], HOLD)
    rows = [pair, fetch(held, far_first)] + other_rows(held)

    passed_keys = fetch(after(far1_keys, near_keys, *rows), beside)
    far2_packed = fetch(after(packed_keys, far1_keys), far_second)
    far2_values = fetch(after(values, far1_keys), far_second)
    first_half, second_half = halve(far1_values)
    passed_first = fetch(first_half, beside)
    passed_second = fetch(after(second_half, far1_keys), beside)

    state = attend_early(
        pattern,
        after(normed_queries, passed_first),
        (normed_keys, near_keys, far1_keys),
        (values, near_values, far1_values),
    )
    inverses, partial, weights = attend_late_keys(
        pattern, normed_queries, passed_keys, far2_packed, rows, state
    )
    return attend_late_values(inverses, partial, weights, (passed_first, passed_second, far2_values))


def solution(mesh):
    in_specs = (
        P(("grp", "frm"), "tp"),
        P(("grp", "frm"), "tp"),
        P(("grp", "frm"), "tp"),
        P("tp"),
        P("tp"),
        P(("grp", "frm"), None),
        P(("grp", "frm"), "tp"),
        P(("grp", "frm"), "tp"),
        P(("grp", "frm")),
    )
    out_specs = P(("grp", "frm"), "tp")
    return jax.shard_map(shards, mesh=mesh, in_specs=in_specs, out_specs=out_specs, check_vma=False)
```

```python
import math

import jax
import jax.numpy as jnp
from jax import lax
from jax.experimental import pallas as pl
from jax.experimental.pallas import tpu as pltpu
from jax.sharding import PartitionSpec as P

HEADS = 20
HEAD_DIM = 128
WINDOW = 2
EPSILON = 1e-06
LANES = 128
SCRATCH_BYTES = 24 * 2**20
DEAD = float("inf")
TO_LOG2 = HEAD_DIM ** (-0.5) * math.log2(math.e)


def fetch(block, source_of, axis="frm"):
    n = lax.axis_size(axis)
    return lax.ppermute(block, axis, [(source_of(i) % n, i) for i in range(n)])


def after(value, *earlier):
    return lax.optimization_barrier((value,) + earlier)[0]


def far_first(i):
    return i + WINDOW if i % 2 == 0 else i - WINDOW


def far_second(i):
    return i - WINDOW if i % 2 == 0 else i + WINDOW


def beside(i):
    return i + 1 if i % 2 == 0 else i - 1


def in_vmem(array):
    return pltpu.with_memory_space_constraint(array, pltpu.VMEM)


def in_hbm(array):
    return pltpu.with_memory_space_constraint(array, pltpu.HBM)


VMEM = pl.BlockSpec(memory_space=pltpu.VMEM)
SMEM = pl.BlockSpec(memory_space=pltpu.SMEM)
PARAMS = pltpu.CompilerParams(vmem_limit_bytes=SCRATCH_BYTES)


CHEAP = pl.CostEstimate(flops=1, transcendentals=0, bytes_accessed=1)

EARLY = pl.CostEstimate(flops=5*10**9, transcendentals=0, bytes_accessed=1)
HOLD = pl.CostEstimate(flops=8 * 10**9, transcendentals=0, bytes_accessed=1)


def head_columns(head):
    return slice(head * HEAD_DIM, (head + 1) * HEAD_DIM)


def score(queries, keys):
    return lax.dot_general(
        queries, keys, (((1,), (1,)), ((), ())), preferred_element_type=jnp.float32
    )


def pack_kernel(live_ref, keys_ref, values_ref, rows_ref, sems):
    slots, features = keys_ref.shape
    copies = [
        pltpu.make_async_copy(keys_ref, rows_ref.at[:, :features], sems.at[0]),
        pltpu.make_async_copy(values_ref, rows_ref.at[:, features:], sems.at[1]),
    ]
    for copy in copies:
        copy.start()
    for copy in copies:
        copy.wait()
    slot = lax.broadcasted_iota(jnp.int32, (slots, features), 0)
    keys = rows_ref[:, :features].astype(jnp.float32)
    rows_ref[:, :features] = jnp.where(slot < live_ref[0], keys, DEAD).astype(jnp.bfloat16)


def pack_rows(live, keys, values):
    slots, features = keys.shape
    return pl.pallas_call(
        pack_kernel,
        out_shape=pltpu.VMEM((slots, 2 * features), jnp.bfloat16),
        in_specs=[SMEM] + [pl.BlockSpec(memory_space=pltpu.HBM)] * 2,
        out_specs=VMEM,
        scratch_shapes=[pltpu.SemaphoreType.DMA((2,))],
        compiler_params=PARAMS,
        cost_estimate=CHEAP,
        name="pack_rows",
    )(live, in_hbm(keys), in_hbm(values))


def load_kernel(*refs):
    sources, loaded = refs[:4], refs[4:8]
    squares_ref, sems = refs[8:]
    copies = [
        pltpu.make_async_copy(source, target, sems.at[i])
        for i, (source, target) in enumerate(zip(sources, loaded))
    ]
    for copy in copies:
        copy.start()
    lane = lax.broadcasted_iota(jnp.int32, squares_ref.shape, 1)
    squares = jnp.zeros(squares_ref.shape, jnp.float32)
    for column, copy in enumerate(copies):
        copy.wait()
        if column < 2:
            rows = loaded[column][...].astype(jnp.float32)
            sums = jnp.sum(rows * rows, axis=1, keepdims=True)
            squares = jnp.where(lane == column, sums, squares)
    squares_ref[...] = squares


def load(queries, keys, gains):
    operands = (queries, keys, *gains)
    return pl.pallas_call(
        load_kernel,
        out_shape=(
            *(pltpu.VMEM(operand.shape, operand.dtype) for operand in operands),
            pltpu.VMEM((queries.shape[0], LANES), jnp.float32),
        ),
        in_specs=[pl.BlockSpec(memory_space=pltpu.HBM)] * 4,
        out_specs=(VMEM,) * 5,
        scratch_shapes=[pltpu.SemaphoreType.DMA((4,))],
        compiler_params=PARAMS,
        cost_estimate=CHEAP,
        name="load",
    )(*map(in_hbm, operands))


def normalized(rows_ref, gain_ref, squares_refs, column):
    square_sum = sum(ref[:, column : column + 1] for ref in squares_refs)
    scale = lax.rsqrt(square_sum / (HEADS * HEAD_DIM) + EPSILON)
    rows = rows_ref[: scale.shape[0]].astype(jnp.float32)
    return (rows * scale * gain_ref[...][None, :]).astype(jnp.bfloat16)


def prepare_kernel(
    queries, keys, query_gain, key_gain, squares, other_squares, query_ref, key_ref
):
    query_ref[...] = normalized(queries, query_gain, (squares, other_squares), 0)
    key_ref[...] = normalized(keys, key_gain, (squares, other_squares), 1)


def prepare(queries, keys, gains, squares):
    return pl.pallas_call(
        prepare_kernel,
        out_shape=(pltpu.VMEM(keys.shape, jnp.bfloat16),) * 2,
        in_specs=[VMEM] * 6,
        out_specs=(VMEM,) * 2,
        compiler_params=PARAMS,
        cost_estimate=CHEAP,
        name="prepare",
    )(*map(in_vmem, (queries, keys, *gains, *squares)))


def attach_kernel(keys_ref, own_rows, other_rows, packed_ref, pair_ref):
    slots = own_rows.shape[0]
    pair_ref[:slots] = own_rows[...]
    pair_ref[slots:] = other_rows[...]
    tokens, features = keys_ref.shape
    packed_ref[:tokens] = keys_ref[...]
    packed_ref[tokens : tokens + 2 * slots] = pair_ref[:, :features]
    packed_ref[tokens + 2 * slots :] = pair_ref[:, features:]


def attach_rows(keys, own_rows, other_rows):
    tokens, features = keys.shape
    count = 2 * own_rows.shape[0]
    return pl.pallas_call(
        attach_kernel,
        out_shape=(
            pltpu.VMEM((tokens + 2 * count, features), jnp.bfloat16),
            pltpu.VMEM((count, 2 * features), jnp.bfloat16),
        ),
        in_specs=[VMEM] * 3,
        out_specs=(VMEM,) * 2,
        compiler_params=PARAMS,
        cost_estimate=CHEAP,
        name="attach_rows",
    )(*map(in_vmem, (keys, own_rows, other_rows)))


def halve_kernel(rows, first_ref, second_ref):
    half = first_ref.shape[0]
    first_ref[...] = rows[:half]
    second_ref[...] = rows[half:]


def halve(rows):
    half = pltpu.VMEM((rows.shape[0] // 2, rows.shape[1]), rows.dtype)
    return pl.pallas_call(
        halve_kernel,
        out_shape=(half, half),
        in_specs=[VMEM],
        out_specs=(VMEM,) * 2,
        compiler_params=PARAMS,
        cost_estimate=CHEAP,
        name="halve",
    )(in_vmem(rows))


def strip_kernel(packed, key_ref):
    key_ref[...] = packed[: key_ref.shape[0]]


def strip(packed, tokens, cost=None):
    return pl.pallas_call(
        strip_kernel,
        out_shape=pltpu.VMEM((tokens, packed.shape[1]), jnp.bfloat16),
        in_specs=[VMEM],
        out_specs=VMEM,
        compiler_params=PARAMS,
        cost_estimate=cost or CHEAP,
        name="strip",
    )(in_vmem(packed))


def pattern_flag(pattern_ref, column):
    even = lax.rem(lax.axis_index("frm"), 2) == 0
    return jnp.where(even, pattern_ref[0, 2 * WINDOW - 1 - column], pattern_ref[0, column]) > 0


def block_bias(flag, tokens):
    return jnp.where(flag, jnp.zeros((1, tokens), jnp.float32), -jnp.inf)


def softmax_parts(scores_ref, head, bias):
    scores = jnp.where(bias < 0, bias, scores_ref[head] * TO_LOG2)
    return scores, jnp.max(scores, axis=1, keepdims=True)


def early_kernel(
    pattern_ref,
    query_ref,
    own_keys,
    near_keys,
    far_keys,
    own_values,
    near_values,
    far_values,
    peaks_ref,
    totals_ref,
    partial_ref,
    scores_ref,
    weights_ref,
):
    tokens, features = query_ref.shape
    heads = features // HEAD_DIM
    bias = jnp.concatenate(
        [
            jnp.zeros((1, tokens), jnp.float32),
            block_bias(pattern_flag(pattern_ref, 1), tokens),
            block_bias(pattern_flag(pattern_ref, 0), tokens),
        ],
        axis=1,
    )
    for head in range(heads):
        columns = head_columns(head)
        keys = [ref[:, columns] for ref in (own_keys, near_keys, far_keys)]
        scores_ref[head] = score(query_ref[:, columns], jnp.concatenate(keys, axis=0))
    for head in range(heads):
        scores, peak = softmax_parts(scores_ref, head, bias)
        weights = jnp.exp2(scores - peak)
        total = jnp.sum(weights, axis=1, keepdims=True)
        weights_ref[head] = weights.astype(jnp.bfloat16)
        peaks_ref[head] = jnp.broadcast_to(peak, (tokens, LANES))
        totals_ref[head] = jnp.broadcast_to(total, (tokens, LANES))
    for head in range(heads):
        columns = head_columns(head)
        values = [ref[:, columns] for ref in (own_values, near_values, far_values)]
        partial_ref[:, columns] = jnp.dot(
            weights_ref[head],
            jnp.concatenate(values, axis=0),
            preferred_element_type=jnp.float32,
        )


def late_keys_kernel(
    pattern_ref,
    query_ref,
    passed_keys,
    far_packed,
    old_peaks_ref,
    old_totals_ref,
    old_partial_ref,
    *refs,
):
    *row_refs, inverses_ref, partial_ref, weights_ref, keys_ref, values_ref, scores_ref = refs
    tokens, features = query_ref.shape
    heads = features // HEAD_DIM
    blocks = 2 * tokens
    keys_ref[:tokens] = passed_keys[...]
    keys_ref[tokens:blocks] = far_packed[:tokens]
    first = 0
    for ref in row_refs:
        count = ref.shape[0]
        keys_ref[blocks + first : blocks + first + count] = ref[:, :features]
        values_ref[first : first + count] = ref[:, features:]
        first += count
    count = (far_packed.shape[0] - tokens) // 2
    keys_ref[blocks + first :] = far_packed[tokens : tokens + count]
    values_ref[first:] = far_packed[tokens + count :]
    marks = score(jnp.ones((8, LANES), jnp.bfloat16), keys_ref[blocks:, :LANES])
    bias = jnp.concatenate(
        [
            block_bias(pattern_flag(pattern_ref, 2), tokens),
            block_bias(pattern_flag(pattern_ref, 3), tokens),
            jnp.where(jnp.abs(marks[:1]) < DEAD, 0.0, -jnp.inf),
        ],
        axis=1,
    )
    for head in range(heads):
        columns = head_columns(head)
        scores_ref[head] = score(query_ref[:, columns], keys_ref[:, columns])
    for head in range(heads):
        columns = head_columns(head)
        scores, peak = softmax_parts(scores_ref, head, bias)
        old_peak = old_peaks_ref[head]
        peak = jnp.maximum(old_peak, peak)
        weights = jnp.exp2(scores - peak[:, :1])
        fading = jnp.exp2(old_peak - peak)
        total = jnp.sum(weights, axis=1, keepdims=True)
        inverse = 1.0 / (old_totals_ref[head] * fading + total)
        inverses_ref[head] = inverse
        weights = weights.astype(jnp.bfloat16)
        weights_ref[head] = weights[:, :blocks]
        product = jnp.dot(
            weights[:, blocks:], values_ref[:, columns], preferred_element_type=jnp.float32
        )
        partial_ref[:, columns] = (old_partial_ref[:, columns] * fading + product) * inverse


def passed_values_kernel(
    inverses_ref, old_partial_ref, weights_ref, first_half, second_half, partial_ref
):
    heads, tokens = weights_ref.shape[:2]
    for head in range(heads):
        columns = head_columns(head)
        values = jnp.concatenate([first_half[:, columns], second_half[:, columns]], axis=0)
        product = jnp.dot(
            weights_ref[head, :, :tokens], values, preferred_element_type=jnp.float32
        )
        partial_ref[:, columns] = old_partial_ref[:, columns] + product * inverses_ref[head]


def late_values_kernel(
    inverses_ref, partial_ref, weights_ref, far_values, out_ref, out_vmem, sems
):
    heads, tokens = weights_ref.shape[:2]
    copies = []
    for head in range(heads):
        columns = head_columns(head)
        product = jnp.dot(
            weights_ref[head, :, tokens:],
            far_values[:, columns],
            preferred_element_type=jnp.float32,
        )
        out_vmem[:, columns] = (
            partial_ref[:, columns] + product * inverses_ref[head]
        ).astype(jnp.bfloat16)
        copy = pltpu.make_async_copy(
            out_vmem.at[:, columns], out_ref.at[:, columns], sems.at[head]
        )
        copy.start()
        copies.append(copy)
    for copy in copies:
        copy.wait()


def attend_early(pattern, queries, keys, values):
    tokens, features = queries.shape
    heads = features // HEAD_DIM
    count = 3 * tokens
    return pl.pallas_call(
        early_kernel,
        out_shape=(
            pltpu.VMEM((heads, tokens, LANES), jnp.float32),
            pltpu.VMEM((heads, tokens, LANES), jnp.float32),
            pltpu.VMEM((tokens, features), jnp.float32),
        ),
        in_specs=[SMEM] + [VMEM] * 7,
        out_specs=(VMEM,) * 3,
        scratch_shapes=[
            pltpu.VMEM((heads, tokens, count), jnp.float32),
            pltpu.VMEM((heads, tokens, count), jnp.bfloat16),
        ],
        compiler_params=PARAMS,
        cost_estimate=EARLY,
        name="attend_early",
    )(pattern, *map(in_vmem, (queries, *keys, *values)))


def attend_late_keys(pattern, queries, passed_keys, far_packed, rows, state):
    tokens, features = queries.shape
    heads = features // HEAD_DIM
    attached = (far_packed.shape[0] - tokens) // 2
    slots = attached + sum(part.shape[0] for part in rows)
    count = 2 * tokens + slots
    operands = (queries, passed_keys, far_packed, *state, *rows)
    return pl.pallas_call(
        late_keys_kernel,
        out_shape=(
            pltpu.VMEM((heads, tokens, LANES), jnp.float32),
            pltpu.VMEM((tokens, features), jnp.float32),
            pltpu.VMEM((heads, tokens, 2 * tokens), jnp.bfloat16),
        ),
        in_specs=[SMEM] + [VMEM] * len(operands),
        out_specs=(VMEM,) * 3,
        scratch_shapes=[
            pltpu.VMEM((count, features), jnp.bfloat16),
            pltpu.VMEM((slots, features), jnp.bfloat16),
            pltpu.VMEM((heads, tokens, count), jnp.float32),
        ],
        compiler_params=PARAMS,
        cost_estimate=CHEAP,
        name="attend_late_keys",
    )(pattern, *map(in_vmem, operands))


def attend_passed_values(inverses, partial, weights, halves):
    return pl.pallas_call(
        passed_values_kernel,
        out_shape=pltpu.VMEM(partial.shape, jnp.float32),
        in_specs=[VMEM] * 5,
        out_specs=VMEM,
        compiler_params=PARAMS,
        cost_estimate=CHEAP,
        name="attend_passed_values",
    )(*map(in_vmem, (inverses, partial, weights, *halves)))


def attend_late_values(inverses, partial, weights, far_values):
    tokens, features = partial.shape
    heads = features // HEAD_DIM
    return pl.pallas_call(
        late_values_kernel,
        out_shape=jax.ShapeDtypeStruct((tokens, features), jnp.bfloat16),
        in_specs=[VMEM] * 4,
        out_specs=pl.BlockSpec(memory_space=pl.ANY),
        scratch_shapes=[
            pltpu.VMEM((tokens, features), jnp.bfloat16),
            pltpu.SemaphoreType.DMA((heads,)),
        ],
        compiler_params=PARAMS,
        cost_estimate=CHEAP,
        name="attend_late_values",
    )(*map(in_vmem, (inverses, partial, weights, far_values)))


def other_rows(pair):
    n = lax.axis_size("frm")
    return [fetch(pair, lambda i: i + distance) for distance in range(4, n - 2, 2)]


def shards(
    queries,
    key_rows,
    values,
    query_gain,
    key_gain,
    pattern,
    reference_keys,
    reference_values,
    reference_live,
):
    tokens = queries.shape[0]
    far1_values = fetch(values, far_first)
    near_values = fetch(values, beside)
    *loaded, squares = load(queries, key_rows, (query_gain, key_gain))
    own_squares = (squares, fetch(squares, lambda i: i ^ 1, "tp"))
    normed_queries, normed_keys = prepare(*loaded[:2], loaded[2:], own_squares)
    near_keys = fetch(normed_keys, beside)
    far1_keys = fetch(normed_keys, far_first)
    own_rows = pack_rows(reference_live, reference_keys, reference_values)
    packed_keys, pair = attach_rows(normed_keys, own_rows, fetch(own_rows, beside))
    held = strip(after(pair, far1_values, near_values), pair.shape[0], HOLD)
    rows = [pair, fetch(held, far_first)] + other_rows(held)

    passed_keys = fetch(after(far1_keys, near_keys, *rows), beside)
    far2_packed = fetch(after(packed_keys, far1_keys), far_second)
    far2_values = fetch(after(values, far1_keys), far_second)
    first_half, second_half = halve(far1_values)
    passed_first = fetch(first_half, beside)
    passed_second = fetch(after(second_half, far1_keys), beside)

    state = attend_early(
        pattern,
        after(normed_queries, passed_first),
        (normed_keys, near_keys, far1_keys),
        (values, near_values, far1_values),
    )
    inverses, partial, weights = attend_late_keys(
        pattern, normed_queries, passed_keys, far2_packed, rows, state
    )
    partial = attend_passed_values(
        inverses, partial, weights, (passed_first, passed_second)
    )
    return attend_late_values(inverses, partial, weights, far2_values)


def solution(mesh):
    in_specs = (
        P(("grp", "frm"), "tp"),
        P(("grp", "frm"), "tp"),
        P(("grp", "frm"), "tp"),
        P("tp"),
        P("tp"),
        P(("grp", "frm"), None),
        P(("grp", "frm"), "tp"),
        P(("grp", "frm"), "tp"),
        P(("grp", "frm")),
    )
    out_specs = P(("grp", "frm"), "tp")
    return jax.shard_map(shards, mesh=mesh, in_specs=in_specs, out_specs=out_specs, check_vma=False)
```
